32 devices in a mesh: freq: 8 (over y, x, core), tile: 4 (over z).
Axes of the slice: x: 2, y: 2, z: 4, core: 2. Of those that a mesh axis runs over, the one named last changes fastest.
Arguments:
- source_field: float32 [2, 8, 64, 1024], P(None, 'freq', 'tile'), may hold values from -6 to 6
- receiver_field: float32 [2, 8, 64, 1024], P(None, 'freq', 'tile'), may hold values from -6 to 6
- velocity_store: float32 [8, 64, 1024], P('freq', 'tile'), may hold values from 0.5 to 1
- slice_owner: int32 [4], replicated, may hold values from 0 to 7, as said below
- region_map: int32 [64, 1024], P('tile', 'freq'), may hold values from 0 to 3, as said below
Outputs:
- wavefields: float32 [2, 2, 8, 64, 1024], P(None, None, 'freq', 'tile')
- smoothed_image: float32 [4, 64, 1024], P(None, 'tile', 'freq')
The draws below stay inside these ranges and needn't reach their ends.
Inputs may be any that keep to these rules, and one draw needn't show every extreme that they name: `slice_owner`: the 4 entries are distinct stored-slice indices; slices 0 and 7 are always among them. `region_map`: labels along the second lateral dimension change at scattered cells.
All inputs are finite; a program needn't handle non-finite values.
Results may differ from the reference program's by a relative error of at most 0.000023.
Values sent between devices are 32-bit elements; how exact they have to be, the bound alone decides.
No kernel may reach another device: no remote copies, remote signals or barrier semaphores. Data moves between devices by JAX's collectives and lax.ppermute only.
A program may use at most 64 MiB of HBM per device.

```python
import math
import jax
import jax.numpy as jnp
from jax import lax

NY = 1024
DEPTHS = 4
SWEEPS = 3
REGIONS = 4
NX = 64
FREQS = 8
SLICES = 8


def draw_slice_owner(key, part):
    middle = 1 + jax.random.permutation(jax.random.fold_in(key, 21), SLICES - 2)[:DEPTHS - 2]
    chosen = jnp.concatenate([jnp.array([0, SLICES - 1], dtype=jnp.int32), middle.astype(jnp.int32)])
    order = jax.random.permutation(jax.random.fold_in(key, 22), DEPTHS)
    return chosen[order].astype(jnp.int32)


def draw_region_map(key, part):
    edges = (jax.random.randint(jax.random.fold_in(key, 11), (NX, NY), 0, 8) == 0).astype(jnp.int32)
    starts = jax.random.randint(jax.random.fold_in(key, 12), (NX, 1), 0, REGIONS)
    return ((jnp.cumsum(edges, axis=1) + starts) % REGIONS).astype(jnp.int32)


def level_of(key, dims, cuts, least, top_value):
    factor_of = 1.0
    for position, blocks in cuts:
        steps = jax.random.uniform(jax.random.fold_in(jax.random.fold_in(key, 6), position), (blocks,), jnp.float32, least / len(cuts), top_value / len(cuts))
        factor_of = factor_of * jnp.repeat(jnp.exp(steps), dims[position] // blocks).reshape((-1,) + (1,) * (len(dims) - 1 - position))
    return factor_of


def centred(key, dims, deviation, reach, pieces=(), kind=jnp.bfloat16):
    loudness = level_of(key, dims, pieces, -0.22, 0.18) if pieces else 1.0
    entries = jax.random.normal(key, dims, jnp.float32) * deviation * loudness
    return jnp.minimum(jnp.maximum(entries, -reach), reach).astype(kind)


def setup_inputs(seed: int = 0) -> dict:
    key_list = jax.random.split(jax.random.key(seed), 6)
    return {
        "source_field": centred(key_list[0], (2, FREQS, NX, NY), 1.0, 6.0, ((1, 8), (2, 4)), jnp.float32),
        "receiver_field": centred(key_list[1], (2, FREQS, NX, NY), 1.0, 6.0, ((1, 8), (2, 4)), jnp.float32),
        "velocity_store": jnp.clip(0.5 + 0.5 * jax.random.uniform(key_list[2], (SLICES, NX, NY), jnp.float32) ** level_of(key_list[2], (SLICES, NX, NY), ((0, 8), (1, 4)), -0.2, 0.2), 0.5, 1.0),
        "slice_owner": draw_slice_owner(jax.random.fold_in(key_list[5], 71), 0),
        "region_map": draw_region_map(jax.random.fold_in(key_list[5], 71), 0),
    }


DAMPING = 0.125
ROTATION = 0.125
STEP_DEPTH = 4.0
SMOOTHING = 0.25

def laplace(wave):
    padded = jnp.pad(wave, ((0, 0), (1, 1), (1, 1)))
    center = padded[:, 1:-1, 1:-1]
    beside_x = padded[:, 2:, 1:-1] + padded[:, :-2, 1:-1]
    beside_y = padded[:, 1:-1, 2:] + padded[:, 1:-1, :-2]
    return beside_x + beside_y - 4.0 * center

def sweep_once(wave, coeff):
    spread = laplace(wave)
    real_part = wave[0] + DAMPING * spread[0] - coeff * spread[1]
    imag_part = wave[1] + DAMPING * spread[1] + coeff * spread[0]
    return jnp.stack([real_part, imag_part])

def rotate(wave, cosines, sines):
    return jnp.stack([wave[0] * cosines - wave[1] * sines, wave[0] * sines + wave[1] * cosines])

def reference(source_field, receiver_field, velocity_store, slice_owner, region_map):
    speeds = jnp.take(velocity_store, slice_owner, axis=0)

    def per_frequency(image_sum, freq_index):
        omega_now = 1.0 + freq_index.astype(jnp.float32) / FREQS
        source_now = lax.dynamic_index_in_dim(source_field, freq_index, 1, keepdims=False)
        receiver_now = lax.dynamic_index_in_dim(receiver_field, freq_index, 1, keepdims=False)
        layers = []
        for depth_no in range(DEPTHS):
            speed_map = speeds[depth_no]
            angles = omega_now * STEP_DEPTH / speed_map
            cosines = jnp.cos(angles)
            sines = jnp.sin(angles)
            source_now = rotate(source_now, cosines, sines)
            receiver_now = rotate(receiver_now, cosines, -sines)
            coeff = ROTATION * speed_map / omega_now
            for sweep_no in range(SWEEPS):
                source_now = sweep_once(source_now, coeff)
                receiver_now = sweep_once(receiver_now, -coeff)
            layers.append(source_now[0] * receiver_now[0] + source_now[1] * receiver_now[1])
        return (image_sum + jnp.stack(layers), jnp.stack([source_now, receiver_now]))
    image_sum, finals = lax.scan(per_frequency, jnp.zeros((DEPTHS, NX, NY), jnp.float32), jnp.arange(FREQS, dtype=jnp.int32))
    wavefields = jnp.moveaxis(finals, 0, 2)
    image_sum = image_sum / math.sqrt(FREQS)
    labels = region_map.astype(jnp.float32) + 1.0
    label_pad = jnp.pad(labels, ((0, 0), (1, 1)))
    image_pad = jnp.pad(image_sum, ((0, 0), (0, 0), (1, 1)))
    next_same = (label_pad[:, 2:] == labels).astype(jnp.float32)
    prev_same = (label_pad[:, :-2] == labels).astype(jnp.float32)
    smoothed = image_sum + SMOOTHING * (next_same * (image_pad[..., 2:] - image_sum) + prev_same * (image_pad[..., :-2] - image_sum))
    return (wavefields, smoothed)
```

```python
import functools
import math

import jax
import jax.numpy as jnp
from jax import lax
from jax.experimental import pallas as pl
from jax.experimental.pallas import tpu as pltpu
from jax.sharding import PartitionSpec as P

SWEEPS = 3
STEP_DEPTH = 4.0
SMOOTHING = 0.25
LANES = 128
SUB = 8
GAIN = 8.0


def tiled_rows(x):
    rows, columns = x.shape[-2:]
    lead = x.shape[:-2]
    x = x.reshape(lead + (rows // SUB, SUB, columns // LANES, LANES))
    return jnp.swapaxes(x, -3, -2).reshape(lead + (-1, LANES))


def untiled_rows(x, rows, columns):
    lead = x.shape[:-2]
    x = x.reshape(lead + (rows // SUB, columns // LANES, SUB, LANES))
    return jnp.swapaxes(x, -3, -2).reshape(lead + (rows, columns))


def tiled_row(r, slabs):
    return pl.ds((r // SUB) * SUB * slabs + r % SUB, slabs, stride=SUB)


def prepare_kernel(halo, src, rcv, vel, lab, own, send_a, send_b, gather):
    _, rows, slabs, _ = own.shape
    for c in range(4):
        field = (src, rcv)[c // 2]
        for r in range(rows):
            own[c, r] = field[c % 2, tiled_row(r, slabs), :]
    even = lax.rem(lax.axis_index("tile"), 2) == 0
    a0 = jnp.where(even, rows - halo, 0)
    b0 = jnp.where(even, 0, rows - halo)
    for c in range(4):
        send_a[c] = own[c, pl.ds(a0, halo)]
        send_b[c] = own[c, pl.ds(b0, halo)]
    gather[: rows * slabs, :] = vel[...]
    gather[rows * slabs :, :] = lab[...].astype(jnp.float32)


def select_kernel(halos, starts, owner, gathered, speeds, send_a, send_b):
    _, rows, slabs, _ = speeds.shape
    even = lax.rem(lax.axis_index("tile"), 2) == 0
    for d, h in enumerate(halos):
        o = owner[d]
        for r in range(rows):
            speeds[d, r] = gathered[o, tiled_row(r, slabs), :]
        a0 = jnp.where(even, rows - h, 0)
        b0 = jnp.where(even, 0, rows - h)
        send_a[starts[d] : starts[d] + h] = speeds[d, pl.ds(a0, h)]
        send_b[starts[d] : starts[d] + h] = speeds[d, pl.ds(b0, h)]


def omega_here(freqs):
    return 1.0 + lax.axis_index("freq").astype(jnp.float32) * (1.0 / freqs)


def sin_cos(x):
    quarter = jnp.floor(x * (2.0 / math.pi) + 0.5)
    r = x - quarter * 1.5703125
    r = r - quarter * 4.837512969970703e-4
    r = r - quarter * 7.549789948768648e-8
    z = r * r
    s = r + r * z * (-1.6666654611e-1 + z * (8.3321608736e-3 - z * 1.9515295891e-4))
    c = 1.0 - 0.5 * z + z * z * (
        4.166664568298827e-2 + z * (-1.388731625493765e-3 + z * 2.443315711809948e-5)
    )
    q = quarter.astype(jnp.int32)
    odd = (q & 1) == 1
    sine = jnp.where(odd, c, s)
    cosine = jnp.where(odd, s, c)
    sine = jnp.where((q & 2) == 2, -sine, sine)
    cosine = jnp.where(((q + 1) & 2) == 2, -cosine, cosine)
    return sine, cosine


def depth_scale(d):
    return 1.0 if d == 0 else GAIN**-SWEEPS


def angles_kernel(freqs, speeds, labels, sines, cosines, ratios, keep_next, keep_prev, pad):
    depths, rows, slabs, _ = speeds.shape
    omega = omega_here(freqs)
    for d in range(depths):

        def row(i, carry, d=d):
            v = speeds[d, pl.ds(i * 4, 4)]
            s, c = sin_cos(omega * STEP_DEPTH / v)
            sines[d, pl.ds(i * 4, 4)] = s * depth_scale(d)
            cosines[d, pl.ds(i * 4, 4)] = c * depth_scale(d)
            ratios[d, pl.ds(i * 4, 4)] = v / omega
            return carry

        lax.fori_loop(0, rows // 4, row, 0)
    pad[...] = jnp.zeros_like(pad)
    mid = labels[...] + 1.0
    pad[:, SUB : SUB + slabs, :] = mid
    after, before = shifted(pad, slice(None))
    keep_next[...] = jnp.where(after == mid, SMOOTHING, 0.0)
    keep_prev[...] = jnp.where(before == mid, SMOOTHING, 0.0)


def shifted(pad, rows):
    slabs = pad.shape[-2] - 2 * SUB
    here = pad[rows, SUB : SUB + slabs, :]
    lane = lax.broadcasted_iota(jnp.int32, here.shape, 2)
    after = jnp.where(lane == 0, pad[rows, SUB + 1 : SUB + 1 + slabs, :], here)
    before = jnp.where(lane == LANES - 1, pad[rows, SUB - 1 : SUB - 1 + slabs, :], here)
    return pltpu.roll(after, LANES - 1, 2), pltpu.roll(before, 1, 2)


def march_kernel(
    freqs, tiles, halos, starts,
    own, field_a, field_b, speed_a, speed_b, sines, cosines, ratios, keep_next, keep_prev,
    waves, image,
    x, y, coef, term,
):
    _, rows, slabs, _ = own.shape
    depths = len(halos)
    halo = halos[0]
    high0 = halo + rows
    extent = high0 + halo
    mid = slice(SUB, SUB + slabs)
    tile = lax.axis_index("tile")
    even = lax.rem(tile, 2) == 0
    at_low = tile == 0
    at_high = tile == tiles - 1
    omega = omega_here(freqs)
    low_in = jnp.where(at_low, 0.0, 1.0)
    high_in = jnp.where(at_high, 0.0, 1.0)

    for buf in (x, y):
        for c in range(4):
            buf[c, :, :SUB, :] = jnp.zeros((extent, SUB, LANES), jnp.float32)
            buf[c, :, SUB + slabs :, :] = jnp.zeros((extent, SUB, LANES), jnp.float32)
    term[...] = jnp.zeros_like(term)

    def unpack(low, high):
        for c in range(4):
            y[c, 0:halo, mid, :] = low[c]
            y[c, high0:extent, mid, :] = high[c]

    @pl.when(even)
    def _():
        unpack(field_b, field_a)

    @pl.when(jnp.logical_not(even))
    def _():
        unpack(field_a, field_b)

    for c in range(4):
        y[c, halo:high0, mid, :] = own[c]

    def rotate(e, n, s, c):
        s0, s1, r0, r1 = (y[k, pl.ds(e, n), mid, :] for k in range(4))
        x[0, pl.ds(e, n), mid, :] = s0 * c - s1 * s
        x[1, pl.ds(e, n), mid, :] = s0 * s + s1 * c
        x[2, pl.ds(e, n), mid, :] = r0 * c + r1 * s
        x[3, pl.ds(e, n), mid, :] = r1 * c - r0 * s

    def sweep(src, dst, k):
        n = 4
        lo, hi = k, extent - k

        def chunk(i, carry):
            e = jnp.minimum(lo + i * n, hi - n)
            ratio = coef[pl.ds(e, n)]
            for pair, sign in ((0, 1.0), (2, -1.0)):
                spread, total = [], []
                for c in (pair, pair + 1):
                    here = src.at[c]
                    q = here[pl.ds(e, n), mid, :] * 4.0
                    after, before = shifted(here, pl.ds(e, n))
                    around = (here[pl.ds(e + 1, n), mid, :] + here[pl.ds(e - 1, n), mid, :]) + (
                        after + before
                    )
                    spread.append(around - q)
                    total.append(around + q)
                if sign > 0:
                    first = total[0] - ratio * spread[1]
                    second = total[1] + ratio * spread[0]
                else:
                    first = total[0] + ratio * spread[1]
                    second = total[1] - ratio * spread[0]
                dst[pair, pl.ds(e, n), mid, :] = first
                dst[pair + 1, pl.ds(e, n), mid, :] = second
            return carry

        lax.fori_loop(0, -(-(hi - lo) // n), chunk, 0)
        for c in range(4):
            dst[c, halo - 1, mid, :] = dst[c, halo - 1, mid, :] * low_in
            dst[c, high0, mid, :] = dst[c, high0, mid, :] * high_in

    for d, h in enumerate(halos):
        scale = depth_scale(d)

        def halo_rows(i, carry, d=d, h=h, scale=scale):
            a = speed_a[starts[d] + i]
            b = speed_b[starts[d] + i]
            for low in (True, False):
                v = jnp.where(even, b, a) if low else jnp.where(even, a, b)
                v = jnp.where(at_low if low else at_high, 1.0, v)
                e = halo - h + i if low else high0 + i
                s, c = sin_cos(omega * STEP_DEPTH / v)
                coef[e] = v / omega
                rotate(e, 1, (s * scale)[None], (c * scale)[None])
            return carry

        lax.fori_loop(0, h, halo_rows, 0)

        def own_rows(i, carry, d=d):
            r = i * 4
            coef[pl.ds(halo + r, 4)] = ratios[d, pl.ds(r, 4)]
            rotate(halo + r, 4, sines[d, pl.ds(r, 4)], cosines[d, pl.ds(r, 4)])
            return carry

        lax.fori_loop(0, rows // 4, own_rows, 0)

        k = d * SWEEPS
        sweep(x, y, k + 1)
        sweep(y, x, k + 2)
        sweep(x, y, k + 3)

        norm = GAIN ** (-2 * SWEEPS) / math.sqrt(freqs)
        s0, s1, r0, r1 = (y[c, halo:high0, mid, :] for c in range(4))
        term[:, mid, :] = (s0 * r0 + s1 * r1) * norm
        here = term[:, mid, :]
        after, before = shifted(term, slice(None))
        smooth = here + (keep_next[...] * (after - here) + keep_prev[...] * (before - here))
        for r in range(rows):
            image[pl.ds(d * rows + r, slabs, stride=depths * rows), :] = smooth[r]

    for c in range(4):
        for r in range(rows):
            waves[c, tiled_row(r, slabs), :] = y[c, halo + r, mid, :] * GAIN**-SWEEPS


def swaps(count, first):
    pairs = [(i, i + 1) for i in range(first, count - 1, 2)]
    return pairs + [(b, a) for a, b in pairs]


def sum_over_freqs(blocks, freqs):
    if freqs % 2 or freqs & (freqs - 1):
        return lax.psum_scatter(blocks, "freq", scatter_dimension=0, tiled=False)
    me = lax.axis_index("freq")
    core, chip = lax.rem(me, 2), me // 2

    def swap(value, bits):
        return lax.ppermute(value, "freq", [(i, i ^ bits) for i in range(freqs)])

    blocks = blocks.reshape((freqs // 2, 2) + blocks.shape[1:])
    kept = lax.dynamic_index_in_dim(blocks, core, 1, keepdims=False)
    sent = lax.dynamic_index_in_dim(blocks, 1 - core, 1, keepdims=False)
    kept = kept + swap(sent, 1)
    total = lax.dynamic_index_in_dim(kept, chip, 0, keepdims=False)
    others = [
        swap(lax.dynamic_index_in_dim(kept, chip ^ m, 0, keepdims=False), 2 * m)
        for m in range(1, freqs // 2)
    ]
    for other in others:
        total = total + other
    return total


def call(kernel, out, scratch=(), name=None, smem=0, operands=0):
    specs = [pl.BlockSpec(memory_space=pltpu.SMEM)] * smem
    specs += [pl.BlockSpec(memory_space=pltpu.VMEM)] * (operands - smem)
    return pl.pallas_call(
        kernel,
        out_shape=[jax.ShapeDtypeStruct(s, jnp.float32) for s in out],
        in_specs=specs,
        out_specs=[pl.BlockSpec(memory_space=pltpu.VMEM)] * len(out),
        scratch_shapes=[pltpu.VMEM(s, jnp.float32) for s in scratch],
        name=name,
    )


def on_device(source_field, receiver_field, velocity_store, slice_owner, region_map):
    freqs, tiles = lax.axis_size("freq"), lax.axis_size("tile")
    _, _, rows, columns = source_field.shape
    slabs = columns // LANES
    depths = slice_owner.shape[0]
    halos = [SWEEPS * (depths - d) for d in range(depths)]
    starts = [sum(halos[:d]) for d in range(depths)]
    halo = halos[0]
    own_columns = region_map.shape[1]
    swap_a = functools.partial(lax.ppermute, axis_name="tile", perm=swaps(tiles, 0))
    swap_b = functools.partial(lax.ppermute, axis_name="tile", perm=swaps(tiles, 1))

    labels = region_map.reshape(-1, LANES)
    vel_rows = rows * slabs
    row = (slabs, LANES)
    own, send_a, send_b, gather = call(
        functools.partial(prepare_kernel, halo),
        [(4, rows) + row, (4, halo) + row, (4, halo) + row, (vel_rows + labels.shape[0], LANES)],
        operands=4,
        name="prepare",
    )(
        tiled_rows(source_field[:, 0]),
        tiled_rows(receiver_field[:, 0]),
        tiled_rows(velocity_store[0]),
        labels,
    )
    field_a, field_b = swap_a(send_a), swap_b(send_b)
    gathered = lax.all_gather(gather, "freq")
    speeds, send_a, send_b = call(
        functools.partial(select_kernel, halos, starts),
        [(depths, rows) + row, (sum(halos),) + row, (sum(halos),) + row],
        smem=1,
        operands=2,
        name="select",
    )(slice_owner, gathered)
    speed_a, speed_b = swap_a(send_a), swap_b(send_b)
    labels = gathered[:, vel_rows:, :].reshape(freqs, rows, own_columns)
    labels = jnp.swapaxes(labels, 0, 1).reshape((rows,) + row)
    table = (depths, rows) + row
    sines, cosines, ratios, keep_next, keep_prev = call(
        functools.partial(angles_kernel, freqs),
        [table, table, table, (rows,) + row, (rows,) + row],
        scratch=[(rows, slabs + 2 * SUB, LANES)],
        operands=2,
        name="angles",
    )(speeds, labels)
    extent = rows + 2 * halo
    padded = (4, extent, slabs + 2 * SUB, LANES)
    waves, image = call(
        functools.partial(march_kernel, freqs, tiles, halos, starts),
        [(4, rows * slabs, LANES), (slabs * depths * rows, LANES)],
        scratch=[padded, padded, (extent,) + row, (rows, slabs + 2 * SUB, LANES)],
        operands=10,
        name="march",
    )(own, field_a, field_b, speed_a, speed_b, sines, cosines, ratios, keep_next, keep_prev)

    if own_columns == LANES:
        blocks = image.reshape(freqs, depths * rows, LANES)
    else:
        blocks = jnp.swapaxes(image.reshape(slabs, depths * rows, LANES), 0, 1)
        blocks = blocks.reshape(depths * rows, freqs, own_columns)
        blocks = jnp.swapaxes(blocks, 0, 1)
    smoothed = sum_over_freqs(blocks, freqs).reshape(depths, rows, own_columns)
    waves = untiled_rows(waves, rows, columns).reshape(2, 2, 1, rows, columns)
    return waves, smoothed


def solution(mesh):
    in_specs = (
        P(None, "freq", "tile", None),
        P(None, "freq", "tile", None),
        P("freq", "tile", None),
        P(),
        P("tile", "freq"),
    )
    out_specs = (P(None, None, "freq", "tile", None), P(None, "tile", "freq"))
    return jax.shard_map(
        on_device, mesh=mesh, in_specs=in_specs, out_specs=out_specs, check_vma=False
    )
```

```python
import functools
import math

import jax
import jax.numpy as jnp
from jax import lax
from jax.experimental import pallas as pl
from jax.experimental.pallas import tpu as pltpu
from jax.sharding import PartitionSpec as P

SWEEPS = 3
STEP_DEPTH = 4.0
SMOOTHING = 0.25
LANES = 128
SUB = 8
GAIN = 8.0


def tiled_rows(x):
    rows, columns = x.shape[-2:]
    lead = x.shape[:-2]
    x = x.reshape(lead + (rows // SUB, SUB, columns // LANES, LANES))
    return jnp.swapaxes(x, -3, -2).reshape(lead + (-1, LANES))


def untiled_rows(x, rows, columns):
    lead = x.shape[:-2]
    x = x.reshape(lead + (rows // SUB, columns // LANES, SUB, LANES))
    return jnp.swapaxes(x, -3, -2).reshape(lead + (rows, columns))


def tiled_row(r, slabs):
    return pl.ds((r // SUB) * SUB * slabs + r % SUB, slabs, stride=SUB)


def prepare_kernel(halo, src, rcv, vel, lab, own, send_a, send_b, gather):
    _, rows, slabs, _ = own.shape
    for c in range(4):
        field = (src, rcv)[c // 2]
        for r in range(rows):
            own[c, r] = field[c % 2, tiled_row(r, slabs), :]
    even = lax.rem(lax.axis_index("tile"), 2) == 0
    a0 = jnp.where(even, rows - halo, 0)
    b0 = jnp.where(even, 0, rows - halo)
    for c in range(4):
        send_a[c] = own[c, pl.ds(a0, halo)]
        send_b[c] = own[c, pl.ds(b0, halo)]
    gather[: rows * slabs, :] = vel[...]
    gather[rows * slabs :, :] = lab[...].astype(jnp.float32)


def select_kernel(halos, starts, owner, gathered, speeds, send_a, send_b):
    _, rows, slabs, _ = speeds.shape
    even = lax.rem(lax.axis_index("tile"), 2) == 0
    for d, h in enumerate(halos):
        o = owner[d]
        for r in range(rows):
            speeds[d, r] = gathered[o, tiled_row(r, slabs), :]
        a0 = jnp.where(even, rows - h, 0)
        b0 = jnp.where(even, 0, rows - h)
        send_a[starts[d] : starts[d] + h] = speeds[d, pl.ds(a0, h)]
        send_b[starts[d] : starts[d] + h] = speeds[d, pl.ds(b0, h)]


def omega_here(freqs):
    return 1.0 + lax.axis_index("freq").astype(jnp.float32) * (1.0 / freqs)


def sin_cos(x):
    quarter = jnp.floor(x * (2.0 / math.pi) + 0.5)
    r = x - quarter * 1.5703125
    r = r - quarter * 4.837512969970703e-4
    r = r - quarter * 7.549789948768648e-8
    z = r * r
    s = r + r * z * (-1.6666654611e-1 + z * (8.3321608736e-3 - z * 1.9515295891e-4))
    c = 1.0 - 0.5 * z + z * z * (
        4.166664568298827e-2 + z * (-1.388731625493765e-3 + z * 2.443315711809948e-5)
    )
    q = quarter.astype(jnp.int32)
    odd = (q & 1) == 1
    sine = jnp.where(odd, c, s)
    cosine = jnp.where(odd, s, c)
    sine = jnp.where((q & 2) == 2, -sine, sine)
    cosine = jnp.where(((q + 1) & 2) == 2, -cosine, cosine)
    return sine, cosine


def depth_scale(d):
    return 1.0 if d == 0 else GAIN**-SWEEPS


def angles_kernel(freqs, speeds, labels, sines, cosines, ratios, keep_next, keep_prev, pad):
    depths, rows, slabs, _ = speeds.shape
    omega = omega_here(freqs)
    for d in range(depths):

        def row(i, carry, d=d):
            v = speeds[d, pl.ds(i * 4, 4)]
            s, c = sin_cos(omega * STEP_DEPTH / v)
            sines[d, pl.ds(i * 4, 4)] = s * depth_scale(d)
            cosines[d, pl.ds(i * 4, 4)] = c * depth_scale(d)
            ratios[d, pl.ds(i * 4, 4)] = v / omega
            return carry

        lax.fori_loop(0, rows // 4, row, 0, unroll=2)
    pad[...] = jnp.zeros_like(pad)
    mid = labels[...] + 1.0
    pad[:, SUB : SUB + slabs, :] = mid
    after, before = shifted(pad, slice(None))
    keep_next[...] = jnp.where(after == mid, SMOOTHING, 0.0)
    keep_prev[...] = jnp.where(before == mid, SMOOTHING, 0.0)


def shifted(pad, rows):
    slabs = pad.shape[-2] - 2 * SUB
    here = pad[rows, SUB : SUB + slabs, :]
    lane = lax.broadcasted_iota(jnp.int32, here.shape, 2)
    after = jnp.where(lane == 0, pad[rows, SUB + 1 : SUB + 1 + slabs, :], here)
    before = jnp.where(lane == LANES - 1, pad[rows, SUB - 1 : SUB - 1 + slabs, :], here)
    return pltpu.roll(after, LANES - 1, 2), pltpu.roll(before, 1, 2)


def march_kernel(
    freqs, tiles, halos, starts,
    own, field_a, field_b, speed_a, speed_b, sines, cosines, ratios, keep_next, keep_prev,
    waves, image,
    x, y, coef, term,
):
    _, rows, slabs, _ = own.shape
    depths = len(halos)
    halo = halos[0]
    high0 = halo + rows
    extent = high0 + halo
    mid = slice(SUB, SUB + slabs)
    tile = lax.axis_index("tile")
    even = lax.rem(tile, 2) == 0
    at_low = tile == 0
    at_high = tile == tiles - 1
    omega = omega_here(freqs)
    low_in = jnp.where(at_low, 0.0, 1.0)
    high_in = jnp.where(at_high, 0.0, 1.0)

    for buf in (x, y):
        for c in range(4):
            buf[c, :, :SUB, :] = jnp.zeros((extent, SUB, LANES), jnp.float32)
            buf[c, :, SUB + slabs :, :] = jnp.zeros((extent, SUB, LANES), jnp.float32)
    term[...] = jnp.zeros_like(term)

    def unpack(low, high):
        for c in range(4):
            y[c, 0:halo, mid, :] = low[c]
            y[c, high0:extent, mid, :] = high[c]

    @pl.when(even)
    def _():
        unpack(field_b, field_a)

    @pl.when(jnp.logical_not(even))
    def _():
        unpack(field_a, field_b)

    for c in range(4):
        y[c, halo:high0, mid, :] = own[c]

    def rotate(e, n, s, c):
        s0, s1, r0, r1 = (y[k, pl.ds(e, n), mid, :] for k in range(4))
        x[0, pl.ds(e, n), mid, :] = s0 * c - s1 * s
        x[1, pl.ds(e, n), mid, :] = s0 * s + s1 * c
        x[2, pl.ds(e, n), mid, :] = r0 * c + r1 * s
        x[3, pl.ds(e, n), mid, :] = r1 * c - r0 * s

    def sweep(src, dst, k):
        n = 2
        lo, hi = k, extent - k

        def chunk(e):
            ratio = coef[pl.ds(e, n)]
            for pair, sign in ((0, 1.0), (2, -1.0)):
                spread, total = [], []
                for c in (pair, pair + 1):
                    here = src.at[c]
                    q = here[pl.ds(e, n), mid, :] * 4.0
                    after, before = shifted(here, pl.ds(e, n))
                    around = (here[pl.ds(e + 1, n), mid, :] + here[pl.ds(e - 1, n), mid, :]) + (
                        after + before
                    )
                    spread.append(around - q)
                    total.append(around + q)
                if sign > 0:
                    first = total[0] - ratio * spread[1]
                    second = total[1] + ratio * spread[0]
                else:
                    first = total[0] + ratio * spread[1]
                    second = total[1] - ratio * spread[0]
                dst[pair, pl.ds(e, n), mid, :] = first
                dst[pair + 1, pl.ds(e, n), mid, :] = second

        for e in range(lo, hi, n):
            chunk(min(e, hi - n))
        for c in range(4):
            dst[c, halo - 1, mid, :] = dst[c, halo - 1, mid, :] * low_in
            dst[c, high0, mid, :] = dst[c, high0, mid, :] * high_in

    for d, h in enumerate(halos):
        scale = depth_scale(d)

        def halo_rows(i, carry, d=d, h=h, scale=scale):
            a = speed_a[starts[d] + i]
            b = speed_b[starts[d] + i]
            for low in (True, False):
                v = jnp.where(even, b, a) if low else jnp.where(even, a, b)
                v = jnp.where(at_low if low else at_high, 1.0, v)
                e = halo - h + i if low else high0 + i
                s, c = sin_cos(omega * STEP_DEPTH / v)
                coef[e] = v / omega
                rotate(e, 1, (s * scale)[None], (c * scale)[None])
            return carry

        lax.fori_loop(0, h, halo_rows, 0, unroll=3)

        def own_rows(i, carry, d=d):
            r = i * 4
            coef[pl.ds(halo + r, 4)] = ratios[d, pl.ds(r, 4)]
            rotate(halo + r, 4, sines[d, pl.ds(r, 4)], cosines[d, pl.ds(r, 4)])
            return carry

        lax.fori_loop(0, rows // 4, own_rows, 0, unroll=True)

        k = d * SWEEPS
        sweep(x, y, k + 1)
        sweep(y, x, k + 2)
        sweep(x, y, k + 3)

        norm = GAIN ** (-2 * SWEEPS) / math.sqrt(freqs)
        s0, s1, r0, r1 = (y[c, halo:high0, mid, :] for c in range(4))
        term[:, mid, :] = (s0 * r0 + s1 * r1) * norm
        here = term[:, mid, :]
        after, before = shifted(term, slice(None))
        smooth = here + (keep_next[...] * (after - here) + keep_prev[...] * (before - here))
        for r in range(rows):
            image[pl.ds(d * rows + r, slabs, stride=depths * rows), :] = smooth[r]

    for c in range(4):
        for r in range(rows):
            waves[c, tiled_row(r, slabs), :] = y[c, halo + r, mid, :] * GAIN**-SWEEPS


def swaps(count, first):
    pairs = [(i, i + 1) for i in range(first, count - 1, 2)]
    return pairs + [(b, a) for a, b in pairs]


def sum_over_freqs(blocks, freqs):
    if freqs % 2 or freqs & (freqs - 1):
        return lax.psum_scatter(blocks, "freq", scatter_dimension=0, tiled=False)
    me = lax.axis_index("freq")
    core, chip = lax.rem(me, 2), me // 2

    def swap(value, bits):
        return lax.ppermute(value, "freq", [(i, i ^ bits) for i in range(freqs)])

    blocks = blocks.reshape((freqs // 2, 2) + blocks.shape[1:])
    kept = lax.dynamic_index_in_dim(blocks, core, 1, keepdims=False)
    sent = lax.dynamic_index_in_dim(blocks, 1 - core, 1, keepdims=False)
    kept = kept + swap(sent, 1)
    total = lax.dynamic_index_in_dim(kept, chip, 0, keepdims=False)
    others = [
        swap(lax.dynamic_index_in_dim(kept, chip ^ m, 0, keepdims=False), 2 * m)
        for m in range(1, freqs // 2)
    ]
    for other in others:
        total = total + other
    return total


def on_chip(x):
    return pltpu.with_memory_space_constraint(x, pltpu.VMEM)


def call(kernel, out, scratch=(), name=None, smem=0, operands=0):
    specs = [pl.BlockSpec(memory_space=pltpu.SMEM)] * smem
    specs += [pl.BlockSpec(memory_space=pltpu.VMEM)] * (operands - smem)
    return pl.pallas_call(
        kernel,
        out_shape=[pltpu.VMEM(s, jnp.float32) for s in out],
        in_specs=specs,
        out_specs=[pl.BlockSpec(memory_space=pltpu.VMEM)] * len(out),
        scratch_shapes=[pltpu.VMEM(s, jnp.float32) for s in scratch],
        name=name,
    )


def on_device(source_field, receiver_field, velocity_store, slice_owner, region_map):
    freqs, tiles = lax.axis_size("freq"), lax.axis_size("tile")
    _, _, rows, columns = source_field.shape
    slabs = columns // LANES
    depths = slice_owner.shape[0]
    halos = [SWEEPS * (depths - d) for d in range(depths)]
    starts = [sum(halos[:d]) for d in range(depths)]
    halo = halos[0]
    own_columns = region_map.shape[1]
    swap_a = functools.partial(lax.ppermute, axis_name="tile", perm=swaps(tiles, 0))
    swap_b = functools.partial(lax.ppermute, axis_name="tile", perm=swaps(tiles, 1))

    labels = region_map.reshape(-1, LANES)
    vel_rows = rows * slabs
    row = (slabs, LANES)
    own, send_a, send_b, gather = call(
        functools.partial(prepare_kernel, halo),
        [(4, rows) + row, (4, halo) + row, (4, halo) + row, (vel_rows + labels.shape[0], LANES)],
        operands=4,
        name="prepare",
    )(
        tiled_rows(source_field[:, 0]),
        tiled_rows(receiver_field[:, 0]),
        tiled_rows(velocity_store[0]),
        labels,
    )
    field_a, field_b = swap_a(send_a), swap_b(send_b)
    gathered = lax.all_gather(gather, "freq")
    speeds, send_a, send_b = call(
        functools.partial(select_kernel, halos, starts),
        [(depths, rows) + row, (sum(halos),) + row, (sum(halos),) + row],
        smem=1,
        operands=2,
        name="select",
    )(slice_owner, on_chip(gathered))
    speed_a, speed_b = swap_a(send_a), swap_b(send_b)
    labels = gathered[:, vel_rows:, :].reshape(freqs, rows, own_columns)
    labels = jnp.swapaxes(labels, 0, 1).reshape((rows,) + row)
    table = (depths, rows) + row
    sines, cosines, ratios, keep_next, keep_prev = call(
        functools.partial(angles_kernel, freqs),
        [table, table, table, (rows,) + row, (rows,) + row],
        scratch=[(rows, slabs + 2 * SUB, LANES)],
        operands=2,
        name="angles",
    )(on_chip(speeds), on_chip(labels))
    extent = rows + 2 * halo
    padded = (4, extent, slabs + 2 * SUB, LANES)
    waves, image = call(
        functools.partial(march_kernel, freqs, tiles, halos, starts),
        [(4, rows * slabs, LANES), (slabs * depths * rows, LANES)],
        scratch=[padded, padded, (extent,) + row, (rows, slabs + 2 * SUB, LANES)],
        operands=10,
        name="march",
    )(
        *map(
            on_chip,
            (own, field_a, field_b, speed_a, speed_b, sines, cosines, ratios, keep_next, keep_prev),
        )
    )

    if own_columns == LANES:
        blocks = image.reshape(freqs, depths * rows, LANES)
    else:
        blocks = jnp.swapaxes(image.reshape(slabs, depths * rows, LANES), 0, 1)
        blocks = blocks.reshape(depths * rows, freqs, own_columns)
        blocks = jnp.swapaxes(blocks, 0, 1)
    smoothed = sum_over_freqs(blocks, freqs).reshape(depths, rows, own_columns)
    waves = untiled_rows(waves, rows, columns).reshape(2, 2, 1, rows, columns)
    return waves, smoothed


def solution(mesh):
    in_specs = (
        P(None, "freq", "tile", None),
        P(None, "freq", "tile", None),
        P("freq", "tile", None),
        P(),
        P("tile", "freq"),
    )
    out_specs = (P(None, None, "freq", "tile", None), P(None, "tile", "freq"))
    return jax.shard_map(
        on_device, mesh=mesh, in_specs=in_specs, out_specs=out_specs, check_vma=False
    )
```

```python
import functools
import math

import jax
import jax.numpy as jnp
from jax import lax
from jax.experimental import pallas as pl
from jax.experimental.pallas import tpu as pltpu
from jax.sharding import PartitionSpec as P

SWEEPS = 3
STEP_DEPTH = 4.0
SMOOTHING = 0.25
LANES = 128
SUB = 8
GAIN = 8.0


def tiled_rows(x):
    rows, columns = x.shape[-2:]
    lead = x.shape[:-2]
    x = x.reshape(lead + (rows // SUB, SUB, columns // LANES, LANES))
    return jnp.swapaxes(x, -3, -2).reshape(lead + (-1, LANES))


def untiled_rows(x, rows, columns):
    lead = x.shape[:-2]
    x = x.reshape(lead + (rows // SUB, columns // LANES, SUB, LANES))
    return jnp.swapaxes(x, -3, -2).reshape(lead + (rows, columns))


def tiled_row(r, slabs):
    return pl.ds((r // SUB) * SUB * slabs + r % SUB, slabs, stride=SUB)


def prepare_kernel(halo, owner, src, rcv, vel, lab, own, send_a, send_b, gather, wanted):
    _, rows, slabs, _ = own.shape
    me = lax.axis_index("freq")
    for d in range(wanted.shape[0]):
        wanted[d] = jnp.full(wanted.shape[1:], (owner[d] ^ me).astype(jnp.float32))
    for c in range(4):
        field = (src, rcv)[c // 2]
        for r in range(rows):
            own[c, r] = field[c % 2, tiled_row(r, slabs), :]
    even = lax.rem(lax.axis_index("tile"), 2) == 0
    a0 = jnp.where(even, rows - halo, 0)
    b0 = jnp.where(even, 0, rows - halo)
    for c in range(4):
        send_a[c] = own[c, pl.ds(a0, halo)]
        send_b[c] = own[c, pl.ds(b0, halo)]
    gather[: rows * slabs, :] = vel[...]
    gather[rows * slabs :, :] = lab[...].astype(jnp.float32)


def select_kernel(halos, starts, wanted, *refs):
    slices, (speeds, send_a, send_b) = refs[:-3], refs[-3:]
    _, rows, slabs, _ = speeds.shape
    even = lax.rem(lax.axis_index("tile"), 2) == 0
    for d, h in enumerate(halos):
        want = wanted[d, :slabs, :]
        hits = [want == float(k) for k in range(1, len(slices))]
        for r in range(rows):
            value = slices[0][tiled_row(r, slabs), :]
            for k, hit in enumerate(hits):
                value = jnp.where(hit, slices[k + 1][tiled_row(r, slabs), :], value)
            speeds[d, r] = value
        a0 = jnp.where(even, rows - h, 0)
        b0 = jnp.where(even, 0, rows - h)
        send_a[starts[d] : starts[d] + h] = speeds[d, pl.ds(a0, h)]
        send_b[starts[d] : starts[d] + h] = speeds[d, pl.ds(b0, h)]


def omega_here(freqs):
    return 1.0 + lax.axis_index("freq").astype(jnp.float32) * (1.0 / freqs)


def sin_cos(x):
    quarter = jnp.floor(x * (2.0 / math.pi) + 0.5)
    r = x - quarter * 1.5703125
    r = r - quarter * 4.837512969970703e-4
    r = r - quarter * 7.549789948768648e-8
    z = r * r
    s = r + r * z * (-1.6666654611e-1 + z * (8.3321608736e-3 - z * 1.9515295891e-4))
    c = 1.0 - 0.5 * z + z * z * (
        4.166664568298827e-2 + z * (-1.388731625493765e-3 + z * 2.443315711809948e-5)
    )
    q = quarter.astype(jnp.int32)
    odd = (q & 1) == 1
    sine = jnp.where(odd, c, s)
    cosine = jnp.where(odd, s, c)
    sine = jnp.where((q & 2) == 2, -sine, sine)
    cosine = jnp.where(((q + 1) & 2) == 2, -cosine, cosine)
    return sine, cosine


def depth_scale(d):
    return 1.0 if d == 0 else GAIN**-SWEEPS


def angles_kernel(freqs, speeds, labels, sines, cosines, ratios, keep_next, keep_prev, pad):
    depths, rows, slabs, _ = speeds.shape
    omega = omega_here(freqs)
    for d in range(depths):

        def row(i, carry, d=d):
            v = speeds[d, pl.ds(i * 4, 4)]
            s, c = sin_cos(omega * STEP_DEPTH / v)
            sines[d, pl.ds(i * 4, 4)] = s * depth_scale(d)
            cosines[d, pl.ds(i * 4, 4)] = c * depth_scale(d)
            ratios[d, pl.ds(i * 4, 4)] = v / omega
            return carry

        lax.fori_loop(0, rows // 4, row, 0, unroll=2)
    pad[...] = jnp.zeros_like(pad)
    mid = labels[...] + 1.0
    pad[:, SUB : SUB + slabs, :] = mid
    after, before = shifted(pad, slice(None))
    keep_next[...] = jnp.where(after == mid, SMOOTHING, 0.0)
    keep_prev[...] = jnp.where(before == mid, SMOOTHING, 0.0)


def shifted(pad, rows):
    slabs = pad.shape[-2] - 2 * SUB
    here = pad[rows, SUB : SUB + slabs, :]
    lane = lax.broadcasted_iota(jnp.int32, here.shape, 2)
    after = jnp.where(lane == 0, pad[rows, SUB + 1 : SUB + 1 + slabs, :], here)
    before = jnp.where(lane == LANES - 1, pad[rows, SUB - 1 : SUB - 1 + slabs, :], here)
    return pltpu.roll(after, LANES - 1, 2), pltpu.roll(before, 1, 2)


def march_kernel(
    freqs, tiles, halos, starts,
    own, field_a, field_b, speed_a, speed_b, sines, cosines, ratios, keep_next, keep_prev,
    waves, image,
    x, y, coef, term,
):
    _, rows, slabs, _ = own.shape
    depths = len(halos)
    halo = halos[0]
    high0 = halo + rows
    extent = high0 + halo
    mid = slice(SUB, SUB + slabs)
    tile = lax.axis_index("tile")
    even = lax.rem(tile, 2) == 0
    at_low = tile == 0
    at_high = tile == tiles - 1
    omega = omega_here(freqs)
    low_in = jnp.where(at_low, 0.0, 1.0)
    high_in = jnp.where(at_high, 0.0, 1.0)

    for buf in (x, y):
        for c in range(4):
            buf[c, :, :SUB, :] = jnp.zeros((extent, SUB, LANES), jnp.float32)
            buf[c, :, SUB + slabs :, :] = jnp.zeros((extent, SUB, LANES), jnp.float32)
    term[...] = jnp.zeros_like(term)

    def unpack(low, high):
        for c in range(4):
            y[c, 0:halo, mid, :] = low[c] * low_in
            y[c, high0:extent, mid, :] = high[c] * high_in

    @pl.when(even)
    def _():
        unpack(field_b, field_a)

    @pl.when(jnp.logical_not(even))
    def _():
        unpack(field_a, field_b)

    for c in range(4):
        y[c, halo:high0, mid, :] = own[c]

    def rotate(e, n, s, c):
        s0, s1, r0, r1 = (y[k, pl.ds(e, n), mid, :] for k in range(4))
        x[0, pl.ds(e, n), mid, :] = s0 * c - s1 * s
        x[1, pl.ds(e, n), mid, :] = s0 * s + s1 * c
        x[2, pl.ds(e, n), mid, :] = r0 * c + r1 * s
        x[3, pl.ds(e, n), mid, :] = r1 * c - r0 * s

    def sweep(src, dst, k):
        n = 2
        lo, hi = k, extent - k

        def chunk(e):
            ratio = coef[pl.ds(e, n)]
            for pair, sign in ((0, 1.0), (2, -1.0)):
                spread, total = [], []
                for c in (pair, pair + 1):
                    here = src.at[c]
                    q = here[pl.ds(e, n), mid, :] * 4.0
                    after, before = shifted(here, pl.ds(e, n))
                    around = (here[pl.ds(e + 1, n), mid, :] + here[pl.ds(e - 1, n), mid, :]) + (
                        after + before
                    )
                    spread.append(around - q)
                    total.append(around + q)
                if sign > 0:
                    first = total[0] - ratio * spread[1]
                    second = total[1] + ratio * spread[0]
                else:
                    first = total[0] + ratio * spread[1]
                    second = total[1] - ratio * spread[0]
                dst[pair, pl.ds(e, n), mid, :] = first
                dst[pair + 1, pl.ds(e, n), mid, :] = second

        for e in range(lo, hi, n):
            chunk(min(e, hi - n))
        for c in range(4):
            dst[c, halo - 1, mid, :] = dst[c, halo - 1, mid, :] * low_in
            dst[c, high0, mid, :] = dst[c, high0, mid, :] * high_in

    for d, h in enumerate(halos):
        scale = depth_scale(d)

        def halo_rows(i, carry, d=d, h=h, scale=scale):
            a = speed_a[starts[d] + i]
            b = speed_b[starts[d] + i]
            for low in (True, False):
                v = jnp.where(even, b, a) if low else jnp.where(even, a, b)
                v = jnp.where(at_low if low else at_high, 1.0, v)
                e = halo - h + i if low else high0 + i
                s, c = sin_cos(omega * STEP_DEPTH / v)
                coef[e] = v / omega
                rotate(e, 1, (s * scale)[None], (c * scale)[None])
            return carry

        lax.fori_loop(0, h, halo_rows, 0, unroll=3)

        def own_rows(i, carry, d=d):
            r = i * 4
            coef[pl.ds(halo + r, 4)] = ratios[d, pl.ds(r, 4)]
            rotate(halo + r, 4, sines[d, pl.ds(r, 4)], cosines[d, pl.ds(r, 4)])
            return carry

        lax.fori_loop(0, rows // 4, own_rows, 0, unroll=True)

        k = d * SWEEPS
        sweep(x, y, k + 1)
        sweep(y, x, k + 2)
        sweep(x, y, k + 3)

        norm = GAIN ** (-2 * SWEEPS) / math.sqrt(freqs)
        s0, s1, r0, r1 = (y[c, halo:high0, mid, :] for c in range(4))
        term[:, mid, :] = (s0 * r0 + s1 * r1) * norm
        here = term[:, mid, :]
        after, before = shifted(term, slice(None))
        smooth = here + (keep_next[...] * (after - here) + keep_prev[...] * (before - here))
        for r in range(rows):
            image[pl.ds(d * rows + r, slabs, stride=depths * rows), :] = smooth[r]

    for c in range(4):
        for r in range(rows):
            waves[c, tiled_row(r, slabs), :] = y[c, halo + r, mid, :] * GAIN**-SWEEPS


def swaps(freqs, tiles, first):
    pairs = []
    for t in range(tiles):
        u = t + 1 if (t - first) % 2 == 0 else t - 1
        for f in range(freqs):
            g = f
            if not 0 <= u < tiles:
                g = min(f ^ 1, freqs - 1)
            pairs.append((f * tiles + t, g * tiles + (u if 0 <= u < tiles else t)))
    return pairs


def from_all_freqs(x, freqs):
    if freqs & (freqs - 1):
        whole = lax.all_gather(x, "freq")
        me = lax.axis_index("freq")
        return [jnp.take(whole, jnp.minimum(me ^ k, freqs - 1), axis=0) for k in range(2 * freqs)]

    def swap(value, bits):
        return lax.ppermute(value, "freq", [(i, i ^ bits) for i in range(freqs)])

    near = [x] + [swap(x, k) for k in range(2, freqs, 2)]
    return [v for x in near for v in (x, swap(x, 1))]


def sum_over_freqs(blocks, freqs):
    if freqs % 2 or freqs & (freqs - 1):
        return lax.psum_scatter(blocks, "freq", scatter_dimension=0, tiled=False)
    me = lax.axis_index("freq")
    core, chip = lax.rem(me, 2), me // 2

    def swap(value, bits):
        return lax.ppermute(value, "freq", [(i, i ^ bits) for i in range(freqs)])

    blocks = blocks.reshape((freqs // 2, 2) + blocks.shape[1:])
    kept = lax.dynamic_index_in_dim(blocks, core, 1, keepdims=False)
    sent = lax.dynamic_index_in_dim(blocks, 1 - core, 1, keepdims=False)
    kept = kept + swap(sent, 1)
    total = lax.dynamic_index_in_dim(kept, chip, 0, keepdims=False)
    others = [
        swap(lax.dynamic_index_in_dim(kept, chip ^ m, 0, keepdims=False), 2 * m)
        for m in range(1, freqs // 2)
    ]
    for other in others:
        total = total + other
    return total


def on_chip(x):
    return pltpu.with_memory_space_constraint(x, pltpu.VMEM)


def call(kernel, out, scratch=(), name=None, smem=0, operands=0):
    specs = [pl.BlockSpec(memory_space=pltpu.SMEM)] * smem
    specs += [pl.BlockSpec(memory_space=pltpu.VMEM)] * (operands - smem)
    return pl.pallas_call(
        kernel,
        out_shape=[pltpu.VMEM(s, jnp.float32) for s in out],
        in_specs=specs,
        out_specs=[pl.BlockSpec(memory_space=pltpu.VMEM)] * len(out),
        scratch_shapes=[pltpu.VMEM(s, jnp.float32) for s in scratch],
        name=name,
    )


def on_device(source_field, receiver_field, velocity_store, slice_owner, region_map):
    freqs, tiles = lax.axis_size("freq"), lax.axis_size("tile")
    _, _, rows, columns = source_field.shape
    slabs = columns // LANES
    depths = slice_owner.shape[0]
    halos = [SWEEPS * (depths - d) for d in range(depths)]
    starts = [sum(halos[:d]) for d in range(depths)]
    halo = halos[0]
    own_columns = region_map.shape[1]
    swap_a = functools.partial(lax.ppermute, axis_name=("freq", "tile"), perm=swaps(freqs, tiles, 0))
    swap_b = functools.partial(lax.ppermute, axis_name=("freq", "tile"), perm=swaps(freqs, tiles, 1))

    labels = region_map.reshape(-1, LANES)
    vel_rows = rows * slabs
    row = (slabs, LANES)
    own, send_a, send_b, gather, wanted = call(
        functools.partial(prepare_kernel, halo),
        [(4, rows) + row, (4, halo) + row, (4, halo) + row, (vel_rows + labels.shape[0], LANES), (depths, SUB, LANES)],
        smem=1,
        operands=5,
        name="prepare",
    )(
        slice_owner,
        tiled_rows(source_field[:, 0]),
        tiled_rows(receiver_field[:, 0]),
        tiled_rows(velocity_store[0]),
        labels,
    )
    field_a, field_b = swap_a(send_a), swap_b(send_b)
    gathered = from_all_freqs(gather, freqs)
    speeds, send_a, send_b = call(
        functools.partial(select_kernel, halos, starts),
        [(depths, rows) + row, (sum(halos),) + row, (sum(halos),) + row],
        operands=1 + len(gathered),
        name="select",
    )(on_chip(wanted), *map(on_chip, gathered))
    speed_a, speed_b = swap_a(send_a), swap_b(send_b)
    me = lax.axis_index("freq")
    labels = jnp.stack([x[vel_rows:, :] for x in gathered[:freqs]])
    labels = labels[jnp.arange(freqs, dtype=jnp.int32) ^ me].reshape(freqs, rows, own_columns)
    labels = jnp.swapaxes(labels, 0, 1).reshape((rows,) + row)
    table = (depths, rows) + row
    sines, cosines, ratios, keep_next, keep_prev = call(
        functools.partial(angles_kernel, freqs),
        [table, table, table, (rows,) + row, (rows,) + row],
        scratch=[(rows, slabs + 2 * SUB, LANES)],
        operands=2,
        name="angles",
    )(on_chip(speeds), on_chip(labels))
    extent = rows + 2 * halo
    padded = (4, extent, slabs + 2 * SUB, LANES)
    waves, image = call(
        functools.partial(march_kernel, freqs, tiles, halos, starts),
        [(4, rows * slabs, LANES), (slabs * depths * rows, LANES)],
        scratch=[padded, padded, (extent,) + row, (rows, slabs + 2 * SUB, LANES)],
        operands=10,
        name="march",
    )(
        *map(
            on_chip,
            (own, field_a, field_b, speed_a, speed_b, sines, cosines, ratios, keep_next, keep_prev),
        )
    )

    if own_columns == LANES:
        blocks = image.reshape(freqs, depths * rows, LANES)
    else:
        blocks = jnp.swapaxes(image.reshape(slabs, depths * rows, LANES), 0, 1)
        blocks = blocks.reshape(depths * rows, freqs, own_columns)
        blocks = jnp.swapaxes(blocks, 0, 1)
    smoothed = sum_over_freqs(blocks, freqs).reshape(depths, rows, own_columns)
    waves = untiled_rows(waves, rows, columns).reshape(2, 2, 1, rows, columns)
    return waves, smoothed


def solution(mesh):
    in_specs = (
        P(None, "freq", "tile", None),
        P(None, "freq", "tile", None),
        P("freq", "tile", None),
        P(),
        P("tile", "freq"),
    )
    out_specs = (P(None, None, "freq", "tile", None), P(None, "tile", "freq"))
    return jax.shard_map(
        on_device, mesh=mesh, in_specs=in_specs, out_specs=out_specs, check_vma=False
    )
```

```python
import functools
import math

import jax
import jax.numpy as jnp
from jax import lax
from jax.experimental import pallas as pl
from jax.experimental.pallas import tpu as pltpu
from jax.sharding import PartitionSpec as P


SWEEPS = 3
STEP_DEPTH = 4.0
SMOOTHING = 0.25
LANES = 128
SUB = 8
GAIN = 8.0


def tiled_rows(x):
    rows, columns = x.shape[-2:]
    lead = x.shape[:-2]
    x = x.reshape(lead + (rows // SUB, SUB, columns // LANES, LANES))
    return jnp.swapaxes(x, -3, -2).reshape(lead + (-1, LANES))


def untiled_rows(x, rows, columns):
    lead = x.shape[:-2]
    x = x.reshape(lead + (rows // SUB, columns // LANES, SUB, LANES))
    return jnp.swapaxes(x, -3, -2).reshape(lead + (rows, columns))


def tiled_row(r, slabs):
    return pl.ds((r // SUB) * SUB * slabs + r % SUB, slabs, stride=SUB)


def prepare_kernel(halo, owner, src, rcv, vel, lab, own, send_a, send_b, gather, wanted):
    _, rows, slabs, _ = own.shape
    me = lax.axis_index("freq")
    for d in range(wanted.shape[0]):
        wanted[d] = jnp.full(wanted.shape[1:], (owner[d] ^ me).astype(jnp.float32))
    for c in range(4):
        field = (src, rcv)[c // 2]
        for r in range(rows):
            own[c, r] = field[c % 2, tiled_row(r, slabs), :]
    even = lax.rem(lax.axis_index("tile"), 2) == 0
    a0 = jnp.where(even, rows - halo, 0)
    b0 = jnp.where(even, 0, rows - halo)
    for c in range(4):
        send_a[c] = own[c, pl.ds(a0, halo)]
        send_b[c] = own[c, pl.ds(b0, halo)]
    gather[: rows * slabs, :] = vel[...]
    gather[rows * slabs :, :] = lab[...].astype(jnp.float32)


def select_kernel(halos, starts, wanted, *refs):
    slices, (speeds, send_a, send_b) = refs[:-3], refs[-3:]
    _, rows, slabs, _ = speeds.shape
    even = lax.rem(lax.axis_index("tile"), 2) == 0
    for d, h in enumerate(halos):
        want = wanted[d, :slabs, :]
        hits = [want == float(k) for k in range(1, len(slices))]
        for r in range(rows):
            value = slices[0][tiled_row(r, slabs), :]
            for k, hit in enumerate(hits):
                value = jnp.where(hit, slices[k + 1][tiled_row(r, slabs), :], value)
            speeds[d, r] = value
        a0 = jnp.where(even, rows - h, 0)
        b0 = jnp.where(even, 0, rows - h)
        send_a[starts[d] : starts[d] + h] = speeds[d, pl.ds(a0, h)]
        send_b[starts[d] : starts[d] + h] = speeds[d, pl.ds(b0, h)]


def omega_here(freqs):
    return 1.0 + lax.axis_index("freq").astype(jnp.float32) * (1.0 / freqs)


def sin_cos(x):
    quarter = jnp.floor(x * (2.0 / math.pi) + 0.5)
    r = x - quarter * 1.5703125
    r = r - quarter * 4.837512969970703e-4
    r = r - quarter * 7.549789948768648e-8
    z = r * r
    s = r + r * z * (-1.6666654611e-1 + z * (8.3321608736e-3 - z * 1.9515295891e-4))
    c = 1.0 - 0.5 * z + z * z * (
        4.166664568298827e-2 + z * (-1.388731625493765e-3 + z * 2.443315711809948e-5)
    )
    q = quarter.astype(jnp.int32)
    odd = (q & 1) == 1
    sine = jnp.where(odd, c, s)
    cosine = jnp.where(odd, s, c)
    sine = jnp.where((q & 2) == 2, -sine, sine)
    cosine = jnp.where(((q + 1) & 2) == 2, -cosine, cosine)
    return sine, cosine


def depth_scale(d):
    return 1.0 if d == 0 else GAIN**-SWEEPS


def angles_kernel(freqs, speeds, labels, sines, cosines, ratios, keep_next, keep_prev, pad):
    depths, rows, slabs, _ = speeds.shape
    omega = omega_here(freqs)
    for d in range(depths):

        def row(i, carry, d=d):
            v = speeds[d, pl.ds(i * 4, 4)]
            s, c = sin_cos(omega * STEP_DEPTH / v)
            sines[d, pl.ds(i * 4, 4)] = s * depth_scale(d)
            cosines[d, pl.ds(i * 4, 4)] = c * depth_scale(d)
            ratios[d, pl.ds(i * 4, 4)] = v / omega
            return carry

        lax.fori_loop(0, rows // 4, row, 0, unroll=2)
    pad[...] = jnp.zeros_like(pad)
    mid = labels[...] + 1.0
    pad[:, SUB : SUB + slabs, :] = mid
    after, before = shifted(pad, slice(None))
    keep_next[...] = jnp.where(after == mid, SMOOTHING, 0.0)
    keep_prev[...] = jnp.where(before == mid, SMOOTHING, 0.0)


def shifted(pad, rows):
    slabs = pad.shape[-2] - 2 * SUB
    here = pad[rows, SUB : SUB + slabs, :]
    lane = lax.broadcasted_iota(jnp.int32, here.shape, 2)
    after = jnp.where(lane == 0, pad[rows, SUB + 1 : SUB + 1 + slabs, :], here)
    before = jnp.where(lane == LANES - 1, pad[rows, SUB - 1 : SUB - 1 + slabs, :], here)
    return pltpu.roll(after, LANES - 1, 2), pltpu.roll(before, 1, 2)


def march_kernel(
    freqs, tiles, halos, starts,
    own, field_a, field_b, speed_a, speed_b, sines, cosines, ratios, keep_next, keep_prev,
    waves, image,
    x, y, coef, term,
):
    _, rows, slabs, _ = own.shape
    depths = len(halos)
    halo = halos[0]
    high0 = halo + rows
    extent = high0 + halo
    mid = slice(SUB, SUB + slabs)
    tile = lax.axis_index("tile")
    even = lax.rem(tile, 2) == 0
    at_low = tile == 0
    at_high = tile == tiles - 1
    omega = omega_here(freqs)
    low_in = jnp.where(at_low, 0.0, 1.0)
    high_in = jnp.where(at_high, 0.0, 1.0)

    for buf in (x, y):
        for c in range(4):
            buf[c, :, :SUB, :] = jnp.zeros((extent, SUB, LANES), jnp.float32)
            buf[c, :, SUB + slabs :, :] = jnp.zeros((extent, SUB, LANES), jnp.float32)
    term[...] = jnp.zeros_like(term)

    def unpack(low, high):
        for c in range(4):
            y[c, 0:halo, mid, :] = low[c] * low_in
            y[c, high0:extent, mid, :] = high[c] * high_in

    @pl.when(even)
    def _():
        unpack(field_b, field_a)

    @pl.when(jnp.logical_not(even))
    def _():
        unpack(field_a, field_b)

    for c in range(4):
        y[c, halo:high0, mid, :] = own[c]

    def rotate(e, n, s, c):
        s0, s1, r0, r1 = (y[k, pl.ds(e, n), mid, :] for k in range(4))
        x[0, pl.ds(e, n), mid, :] = s0 * c - s1 * s
        x[1, pl.ds(e, n), mid, :] = s0 * s + s1 * c
        x[2, pl.ds(e, n), mid, :] = r0 * c + r1 * s
        x[3, pl.ds(e, n), mid, :] = r1 * c - r0 * s

    def sweep(src, dst, k):
        n = 2
        lo, hi = k, extent - k

        def chunk(e):
            ratio = coef[pl.ds(e, n)]
            for pair, sign in ((0, 1.0), (2, -1.0)):
                spread, total = [], []
                for c in (pair, pair + 1):
                    here = src.at[c]
                    q = here[pl.ds(e, n), mid, :] * 4.0
                    after, before = shifted(here, pl.ds(e, n))
                    around = (here[pl.ds(e + 1, n), mid, :] + here[pl.ds(e - 1, n), mid, :]) + (
                        after + before
                    )
                    spread.append(around - q)
                    total.append(around + q)
                if sign > 0:
                    first = total[0] - ratio * spread[1]
                    second = total[1] + ratio * spread[0]
                else:
                    first = total[0] + ratio * spread[1]
                    second = total[1] - ratio * spread[0]
                dst[pair, pl.ds(e, n), mid, :] = first
                dst[pair + 1, pl.ds(e, n), mid, :] = second

        for e in range(lo, hi, n):
            chunk(min(e, hi - n))
        for c in range(4):
            dst[c, halo - 1, mid, :] = dst[c, halo - 1, mid, :] * low_in
            dst[c, high0, mid, :] = dst[c, high0, mid, :] * high_in

    for d, h in enumerate(halos):
        scale = depth_scale(d)

        def halo_rows(i, carry, d=d, h=h, scale=scale):
            a = speed_a[starts[d] + i]
            b = speed_b[starts[d] + i]
            for low in (True, False):
                v = jnp.where(even, b, a) if low else jnp.where(even, a, b)
                v = jnp.where(at_low if low else at_high, 1.0, v)
                e = halo - h + i if low else high0 + i
                s, c = sin_cos(omega * STEP_DEPTH / v)
                coef[e] = v / omega
                rotate(e, 1, (s * scale)[None], (c * scale)[None])
            return carry

        lax.fori_loop(0, h, halo_rows, 0, unroll=3)

        def own_rows(i, carry, d=d):
            r = i * 4
            coef[pl.ds(halo + r, 4)] = ratios[d, pl.ds(r, 4)]
            rotate(halo + r, 4, sines[d, pl.ds(r, 4)], cosines[d, pl.ds(r, 4)])
            return carry

        lax.fori_loop(0, rows // 4, own_rows, 0, unroll=True)

        k = d * SWEEPS
        sweep(x, y, k + 1)
        sweep(y, x, k + 2)
        sweep(x, y, k + 3)

        norm = GAIN ** (-2 * SWEEPS) / math.sqrt(freqs)
        s0, s1, r0, r1 = (y[c, halo:high0, mid, :] for c in range(4))
        term[:, mid, :] = (s0 * r0 + s1 * r1) * norm
        here = term[:, mid, :]
        after, before = shifted(term, slice(None))
        smooth = here + (keep_next[...] * (after - here) + keep_prev[...] * (before - here))
        for r in range(rows):
            image[pl.ds(d * rows + r, slabs, stride=depths * rows), :] = smooth[r]

    for c in range(4):
        for r in range(rows):
            waves[c, tiled_row(r, slabs), :] = y[c, halo + r, mid, :] * GAIN**-SWEEPS


def swaps(freqs, tiles, first):
    pairs = []
    for t in range(tiles):
        u = t + 1 if (t - first) % 2 == 0 else t - 1
        for f in range(freqs):
            g = f
            if not 0 <= u < tiles:
                g = min(f ^ 1, freqs - 1)
            pairs.append((f * tiles + t, g * tiles + (u if 0 <= u < tiles else t)))
    return pairs


def from_all_freqs(x, freqs):
    if freqs & (freqs - 1):
        whole = lax.all_gather(x, "freq")
        me = lax.axis_index("freq")
        return [jnp.take(whole, jnp.minimum(me ^ k, freqs - 1), axis=0) for k in range(2 * freqs)]

    def swap(value, bits):
        return lax.ppermute(value, "freq", [(i, i ^ bits) for i in range(freqs)])

    near = [x]
    for k in range(2, freqs, 2):
        near.append(swap(x, k))
    return [v for x in near for v in (x, swap(x, 1))]


def sum_over_freqs(blocks, freqs):
    if freqs % 2 or freqs & (freqs - 1):
        return lax.psum_scatter(blocks, "freq", scatter_dimension=0, tiled=False)
    me = lax.axis_index("freq")
    core, chip = lax.rem(me, 2), me // 2

    def swap(value, bits):
        return lax.ppermute(value, "freq", [(i, i ^ bits) for i in range(freqs)])

    blocks = blocks.reshape((freqs // 2, 2) + blocks.shape[1:])
    kept = lax.dynamic_index_in_dim(blocks, core, 1, keepdims=False)
    sent = lax.dynamic_index_in_dim(blocks, 1 - core, 1, keepdims=False)
    kept = kept + swap(sent, 1)
    total = lax.dynamic_index_in_dim(kept, chip, 0, keepdims=False)
    others = []
    for m in range(1, freqs // 2):
        others.append(swap(lax.dynamic_index_in_dim(kept, chip ^ m, 0, keepdims=False), 2 * m))
    for other in others:
        total = total + other
    return total


def on_chip(x):
    return pltpu.with_memory_space_constraint(x, pltpu.VMEM)


def call(kernel, out, scratch=(), smem=0, operands=0):
    specs = [pl.BlockSpec(memory_space=pltpu.SMEM)] * smem
    specs += [pl.BlockSpec(memory_space=pltpu.VMEM)] * (operands - smem)
    return pl.pallas_call(
        kernel,
        out_shape=[pltpu.VMEM(s, jnp.float32) for s in out],
        in_specs=specs,
        out_specs=[pl.BlockSpec(memory_space=pltpu.VMEM)] * len(out),
        scratch_shapes=[pltpu.VMEM(s, jnp.float32) for s in scratch],
    )


def on_device(source_field, receiver_field, velocity_store, slice_owner, region_map):
    freqs, tiles = lax.axis_size("freq"), lax.axis_size("tile")
    _, _, rows, columns = source_field.shape
    slabs = columns // LANES
    depths = slice_owner.shape[0]
    halos = [SWEEPS * (depths - d) for d in range(depths)]
    starts = [sum(halos[:d]) for d in range(depths)]
    halo = halos[0]
    own_columns = region_map.shape[1]
    swap_a = functools.partial(lax.ppermute, axis_name=("freq", "tile"), perm=swaps(freqs, tiles, 0))
    swap_b = functools.partial(lax.ppermute, axis_name=("freq", "tile"), perm=swaps(freqs, tiles, 1))

    labels = region_map.reshape(-1, LANES)
    vel_rows = rows * slabs
    row = (slabs, LANES)
    own, send_a, send_b, gather, wanted = call(
        functools.partial(prepare_kernel, halo),
        [(4, rows) + row, (4, halo) + row, (4, halo) + row, (vel_rows + labels.shape[0], LANES), (depths, SUB, LANES)],
        smem=1,
        operands=5,
    )(
        slice_owner,
        tiled_rows(source_field[:, 0]),
        tiled_rows(receiver_field[:, 0]),
        tiled_rows(velocity_store[0]),
        labels,
    )
    field_a, field_b = swap_a(send_a), swap_b(send_b)
    gathered = from_all_freqs(gather, freqs)
    speeds, send_a, send_b = call(
        functools.partial(select_kernel, halos, starts),
        [(depths, rows) + row, (sum(halos),) + row, (sum(halos),) + row],
        operands=1 + len(gathered),
    )(on_chip(wanted), *map(on_chip, gathered))
    speed_a = swap_a(send_a)
    speed_b = swap_b(send_b)
    me = lax.axis_index("freq")
    labels = jnp.stack([x[vel_rows:, :] for x in gathered[:freqs]])
    labels = labels[jnp.arange(freqs, dtype=jnp.int32) ^ me].reshape(freqs, rows, own_columns)
    labels = jnp.swapaxes(labels, 0, 1).reshape((rows,) + row)
    table = (depths, rows) + row
    sines, cosines, ratios, keep_next, keep_prev = call(
        functools.partial(angles_kernel, freqs),
        [table, table, table, (rows,) + row, (rows,) + row],
        scratch=[(rows, slabs + 2 * SUB, LANES)],
        operands=2,
    )(on_chip(speeds), on_chip(labels))
    extent = rows + 2 * halo
    padded = (4, extent, slabs + 2 * SUB, LANES)
    waves, image = call(
        functools.partial(march_kernel, freqs, tiles, halos, starts),
        [(4, rows * slabs, LANES), (slabs * depths * rows, LANES)],
        scratch=[padded, padded, (extent,) + row, (rows, slabs + 2 * SUB, LANES)],
        operands=10,
    )(
        *map(
            on_chip,
            (own, field_a, field_b, speed_a, speed_b, sines, cosines, ratios, keep_next, keep_prev),
        )
    )

    if own_columns == LANES:
        blocks = image.reshape(freqs, depths * rows, LANES)
    else:
        blocks = jnp.swapaxes(image.reshape(slabs, depths * rows, LANES), 0, 1)
        blocks = blocks.reshape(depths * rows, freqs, own_columns)
        blocks = jnp.swapaxes(blocks, 0, 1)
    smoothed = sum_over_freqs(blocks, freqs).reshape(depths, rows, own_columns)
    waves = untiled_rows(waves, rows, columns).reshape(2, 2, 1, rows, columns)
    return waves, smoothed


def solution(mesh):
    in_specs = (
        P(None, "freq", "tile", None),
        P(None, "freq", "tile", None),
        P("freq", "tile", None),
        P(),
        P("tile", "freq"),
    )
    out_specs = (P(None, None, "freq", "tile", None), P(None, "tile", "freq"))

    return jax.shard_map(on_device, mesh=mesh, in_specs=in_specs, out_specs=out_specs, check_vma=False)
```

```python
import functools
import math

import jax
import jax.numpy as jnp
from jax import lax
from jax.experimental import pallas as pl
from jax.experimental.pallas import tpu as pltpu
from jax.sharding import PartitionSpec as P


SWEEPS = 3
STEP_DEPTH = 4.0
SMOOTHING = 0.25
LANES = 128
SUB = 8
GAIN = 8.0
VMEM_LIMIT = 24 * 2**20


def tiled_rows(x):
    rows, columns = x.shape[-2:]
    lead = x.shape[:-2]
    x = x.reshape(lead + (rows // SUB, SUB, columns // LANES, LANES))
    return jnp.swapaxes(x, -3, -2).reshape(lead + (-1, LANES))


def untiled_rows(x, rows, columns):
    lead = x.shape[:-2]
    x = x.reshape(lead + (rows // SUB, columns // LANES, SUB, LANES))
    return jnp.swapaxes(x, -3, -2).reshape(lead + (rows, columns))


def tiled_row(r, slabs):
    return pl.ds((r // SUB) * SUB * slabs + r % SUB, slabs, stride=SUB)


def prepare_kernel(halo, owner, src, rcv, vel, lab, own, send_a, send_b, gather, wanted):
    _, rows, slabs, _ = own.shape
    me = lax.axis_index("freq")
    for d in range(wanted.shape[0]):
        wanted[d] = jnp.full(wanted.shape[1:], (owner[d] ^ me).astype(jnp.float32))
    for c in range(4):
        field = (src, rcv)[c // 2]
        for r in range(rows):
            own[c, r] = field[c % 2, tiled_row(r, slabs), :]
    even = lax.rem(lax.axis_index("tile"), 2) == 0
    a0 = jnp.where(even, rows - halo, 0)
    b0 = jnp.where(even, 0, rows - halo)
    for c in range(4):
        send_a[c] = own[c, pl.ds(a0, halo)]
        send_b[c] = own[c, pl.ds(b0, halo)]
    gather[: rows * slabs, :] = vel[...]
    gather[rows * slabs :, :] = lab[...].astype(jnp.float32)


def select_kernel(halos, starts, wanted, *refs):
    slices, (speeds, send_a, send_b) = refs[:-3], refs[-3:]
    _, rows, slabs, _ = speeds.shape
    even = lax.rem(lax.axis_index("tile"), 2) == 0
    for d, h in enumerate(halos):
        want = wanted[d, :slabs, :]
        hits = [want == float(k) for k in range(1, len(slices))]
        for r in range(rows):
            value = slices[0][tiled_row(r, slabs), :]
            for k, hit in enumerate(hits):
                value = jnp.where(hit, slices[k + 1][tiled_row(r, slabs), :], value)
            speeds[d, r] = value
        a0 = jnp.where(even, rows - h, 0)
        b0 = jnp.where(even, 0, rows - h)
        send_a[starts[d] : starts[d] + h] = speeds[d, pl.ds(a0, h)]
        send_b[starts[d] : starts[d] + h] = speeds[d, pl.ds(b0, h)]


def omega_here(freqs):
    return 1.0 + lax.axis_index("freq").astype(jnp.float32) * (1.0 / freqs)


def sin_cos(x):
    quarter = jnp.floor(x * (2.0 / math.pi) + 0.5)
    r = x - quarter * 1.5703125
    r = r - quarter * 4.837512969970703e-4
    r = r - quarter * 7.549789948768648e-8
    z = r * r
    s = r + r * z * (-1.6666654611e-1 + z * (8.3321608736e-3 - z * 1.9515295891e-4))
    c = 1.0 - 0.5 * z + z * z * (
        4.166664568298827e-2 + z * (-1.388731625493765e-3 + z * 2.443315711809948e-5)
    )
    q = quarter.astype(jnp.int32)
    odd = (q & 1) == 1
    sine = jnp.where(odd, c, s)
    cosine = jnp.where(odd, s, c)
    sine = jnp.where((q & 2) == 2, -sine, sine)
    cosine = jnp.where(((q + 1) & 2) == 2, -cosine, cosine)
    return sine, cosine


def depth_scale(d):
    return 1.0 if d == 0 else GAIN**-SWEEPS


def angles_kernel(freqs, speeds, labels, sines, cosines, ratios, keep_next, keep_prev, pad):
    depths, rows, slabs, _ = speeds.shape
    omega = omega_here(freqs)
    for d in range(depths):

        def row(i, carry, d=d):
            v = speeds[d, pl.ds(i * 4, 4)]
            s, c = sin_cos(omega * STEP_DEPTH / v)
            sines[d, pl.ds(i * 4, 4)] = s * depth_scale(d)
            cosines[d, pl.ds(i * 4, 4)] = c * depth_scale(d)
            ratios[d, pl.ds(i * 4, 4)] = v / omega
            return carry

        lax.fori_loop(0, rows // 4, row, 0, unroll=2)
    pad[...] = jnp.zeros_like(pad)
    mid = labels[...] + 1.0
    pad[:, SUB : SUB + slabs, :] = mid
    after, before = shifted(pad, slice(None))
    keep_next[...] = jnp.where(after == mid, SMOOTHING, 0.0)
    keep_prev[...] = jnp.where(before == mid, SMOOTHING, 0.0)


def shifted(pad, rows):
    slabs = pad.shape[-2] - 2 * SUB
    here = pad[rows, SUB : SUB + slabs, :]
    lane = lax.broadcasted_iota(jnp.int32, here.shape, 2)
    after = jnp.where(lane == 0, pad[rows, SUB + 1 : SUB + 1 + slabs, :], here)
    before = jnp.where(lane == LANES - 1, pad[rows, SUB - 1 : SUB - 1 + slabs, :], here)
    return pltpu.roll(after, LANES - 1, 2), pltpu.roll(before, 1, 2)


def rotate(src, dst, e, n, s, c):
    slabs = src.shape[-2] - 2 * SUB
    mid = slice(SUB, SUB + slabs)
    s0, s1, r0, r1 = (src[k, pl.ds(e, n), mid, :] for k in range(4))
    dst[0, pl.ds(e, n), mid, :] = s0 * c - s1 * s
    dst[1, pl.ds(e, n), mid, :] = s0 * s + s1 * c
    dst[2, pl.ds(e, n), mid, :] = r0 * c + r1 * s
    dst[3, pl.ds(e, n), mid, :] = r1 * c - r0 * s


def sweep_rows(src, dst, ratio_of, lo, hi):
    n = 2
    slabs = src.shape[-2] - 2 * SUB
    mid = slice(SUB, SUB + slabs)

    def chunk(e):
        ratio = ratio_of(e, n)
        for pair, sign in ((0, 1.0), (2, -1.0)):
            spread, total = [], []
            for c in (pair, pair + 1):
                here = src.at[c]
                q = here[pl.ds(e, n), mid, :] * 4.0
                after, before = shifted(here, pl.ds(e, n))
                around = (here[pl.ds(e + 1, n), mid, :] + here[pl.ds(e - 1, n), mid, :]) + (
                    after + before
                )
                spread.append(around - q)
                total.append(around + q)
            if sign > 0:
                first = total[0] - ratio * spread[1]
                second = total[1] + ratio * spread[0]
            else:
                first = total[0] + ratio * spread[1]
                second = total[1] - ratio * spread[0]
            dst[pair, pl.ds(e, n), mid, :] = first
            dst[pair + 1, pl.ds(e, n), mid, :] = second

    for e in range(lo, hi, n):
        chunk(min(e, hi - n))


def image_term(y, lo, hi, freqs):
    slabs = y.shape[-2] - 2 * SUB
    norm = GAIN ** (-2 * SWEEPS) / math.sqrt(freqs)
    s0, s1, r0, r1 = (y[c, lo:hi, SUB : SUB + slabs, :] for c in range(4))
    return (s0 * r0 + s1 * r1) * norm


def begin_kernel(
    freqs, tiles, halos, own, field_a, field_b, sines, cosines, ratios, x, y, z, early
):
    _, rows, slabs, _ = own.shape
    halo = halos[0]
    high0 = halo + rows
    extent = high0 + halo
    mid = slice(SUB, SUB + slabs)
    tile = lax.axis_index("tile")
    even = lax.rem(tile, 2) == 0
    low_in = jnp.where(tile == 0, 0.0, 1.0)
    high_in = jnp.where(tile == tiles - 1, 0.0, 1.0)

    for buf in (x, y, z):
        for c in range(4):
            buf[c, :, :SUB, :] = jnp.zeros((extent, SUB, LANES), jnp.float32)
            buf[c, :, SUB + slabs :, :] = jnp.zeros((extent, SUB, LANES), jnp.float32)

    def unpack(low, high):
        for c in range(4):
            y[c, 0:halo, mid, :] = low[c] * low_in
            y[c, high0:extent, mid, :] = high[c] * high_in

    @pl.when(even)
    def _():
        unpack(field_b, field_a)

    @pl.when(jnp.logical_not(even))
    def _():
        unpack(field_a, field_b)

    for c in range(4):
        y[c, halo:high0, mid, :] = own[c]

    for d in range(len(halos)):
        k = d * SWEEPS
        turned = (x, z)[d % 2]
        if 2 * k >= rows:
            break
        for r in range(k, rows - k, 2):
            at = slice(r, r + 2)
            rotate(y, turned, halo + r, 2, sines[d, at], cosines[d, at])
        for src, dst in ((turned, y), (y, turned), (turned, y)):
            k += 1
            if 2 * k < rows:
                ratio_of = lambda e, n, d=d: ratios[d, pl.ds(e - halo, n)]
                sweep_rows(src, dst, ratio_of, halo + k, high0 - k)
        if 2 * k < rows:
            early[d, k : rows - k] = image_term(y, halo + k, high0 - k, freqs)


def march_kernel(
    freqs, tiles, halos, starts,
    x_in, y_in, z_in, early, speed_a, speed_b, sines, cosines, ratios, keep_next, keep_prev,
    x, y, z, waves, image,
    coef, term,
):
    _, rows, slabs, _ = sines.shape
    depths = len(halos)
    halo = halos[0]
    high0 = halo + rows
    extent = high0 + halo
    mid = slice(SUB, SUB + slabs)
    tile = lax.axis_index("tile")
    even = lax.rem(tile, 2) == 0
    at_low = tile == 0
    at_high = tile == tiles - 1
    omega = omega_here(freqs)
    low_in = jnp.where(at_low, 0.0, 1.0)
    high_in = jnp.where(at_high, 0.0, 1.0)
    term[...] = jnp.zeros_like(term)

    def sweep(src, dst, k):
        ratio_of = lambda e, n: coef[pl.ds(e, n)]
        if 2 * k < rows:
            sweep_rows(src, dst, ratio_of, k, halo + k)
            sweep_rows(src, dst, ratio_of, high0 - k, extent - k)
        else:
            sweep_rows(src, dst, ratio_of, k, extent - k)
        for c in range(4):
            dst[c, halo - 1, mid, :] = dst[c, halo - 1, mid, :] * low_in
            dst[c, high0, mid, :] = dst[c, high0, mid, :] * high_in

    for d, h in enumerate(halos):
        scale = depth_scale(d)
        turned = (x, z)[d % 2]

        def halo_rows(i, carry, d=d, h=h, scale=scale, turned=turned):
            a = speed_a[starts[d] + i]
            b = speed_b[starts[d] + i]
            for low in (True, False):
                v = jnp.where(even, b, a) if low else jnp.where(even, a, b)
                v = jnp.where(at_low if low else at_high, 1.0, v)
                e = halo - h + i if low else high0 + i
                s, c = sin_cos(omega * STEP_DEPTH / v)
                coef[e] = v / omega
                rotate(y, turned, e, 1, (s * scale)[None], (c * scale)[None])
            return carry

        lax.fori_loop(0, h, halo_rows, 0, unroll=3)
        coef[halo:high0] = ratios[d]
        k = d * SWEEPS
        for r in range(rows):
            if r < k or r >= rows - k:
                rotate(y, turned, halo + r, 1, sines[d, r : r + 1], cosines[d, r : r + 1])

        sweep(turned, y, k + 1)
        sweep(y, turned, k + 2)
        sweep(turned, y, k + 3)

        k += SWEEPS
        if 2 * k < rows:
            term[:k, mid, :] = image_term(y, halo, halo + k, freqs)
            term[k : rows - k, mid, :] = early[d, k : rows - k]
            term[rows - k :, mid, :] = image_term(y, high0 - k, high0, freqs)
        else:
            term[:, mid, :] = image_term(y, halo, high0, freqs)
        here = term[:, mid, :]
        after, before = shifted(term, slice(None))
        smooth = here + (keep_next[...] * (after - here) + keep_prev[...] * (before - here))
        for r in range(rows):
            image[pl.ds(d * rows + r, slabs, stride=depths * rows), :] = smooth[r]

    for c in range(4):
        for r in range(rows):
            waves[c, tiled_row(r, slabs), :] = y[c, halo + r, mid, :] * GAIN**-SWEEPS


def swaps(freqs, tiles, first):
    pairs = []
    for t in range(tiles):
        u = t + 1 if (t - first) % 2 == 0 else t - 1
        for f in range(freqs):
            g = f
            if not 0 <= u < tiles:
                g = min(f ^ 1, freqs - 1)
            pairs.append((f * tiles + t, g * tiles + (u if 0 <= u < tiles else t)))
    return pairs


def from_all_freqs(x, freqs):
    if freqs & (freqs - 1):
        whole = lax.all_gather(x, "freq")
        me = lax.axis_index("freq")
        return [jnp.take(whole, jnp.minimum(me ^ k, freqs - 1), axis=0) for k in range(2 * freqs)]

    def swap(value, bits):
        return lax.ppermute(value, "freq", [(i, i ^ bits) for i in range(freqs)])

    near = [x]
    for k in range(2, freqs, 2):
        near.append(swap(x, k))
    return [v for x in near for v in (x, swap(x, 1))]


def sum_over_freqs(blocks, freqs):
    if freqs % 2 or freqs & (freqs - 1):
        return lax.psum_scatter(blocks, "freq", scatter_dimension=0, tiled=False)
    me = lax.axis_index("freq")
    core, chip = lax.rem(me, 2), me // 2

    def swap(value, bits):
        return lax.ppermute(value, "freq", [(i, i ^ bits) for i in range(freqs)])

    blocks = blocks.reshape((freqs // 2, 2) + blocks.shape[1:])
    kept = lax.dynamic_index_in_dim(blocks, core, 1, keepdims=False)
    sent = lax.dynamic_index_in_dim(blocks, 1 - core, 1, keepdims=False)
    kept = kept + swap(sent, 1)
    total = lax.dynamic_index_in_dim(kept, chip, 0, keepdims=False)
    others = []
    for m in range(1, freqs // 2):
        others.append(swap(lax.dynamic_index_in_dim(kept, chip ^ m, 0, keepdims=False), 2 * m))
    for other in others:
        total = total + other
    return total


def on_chip(x):
    return pltpu.with_memory_space_constraint(x, pltpu.VMEM)


def call(kernel, out, scratch=(), name=None, smem=0, operands=0, aliases=None):
    specs = [pl.BlockSpec(memory_space=pltpu.SMEM)] * smem
    specs += [pl.BlockSpec(memory_space=pltpu.VMEM)] * (operands - smem)
    return pl.pallas_call(
        kernel,
        out_shape=[pltpu.VMEM(s, jnp.float32) for s in out],
        in_specs=specs,
        out_specs=[pl.BlockSpec(memory_space=pltpu.VMEM)] * len(out),
        scratch_shapes=[pltpu.VMEM(s, jnp.float32) for s in scratch],
        input_output_aliases=aliases or {},
        compiler_params=None if name == 'prepare' else pltpu.CompilerParams(vmem_limit_bytes=VMEM_LIMIT),
    )


def on_device(source_field, receiver_field, velocity_store, slice_owner, region_map):
    freqs, tiles = lax.axis_size("freq"), lax.axis_size("tile")
    _, _, rows, columns = source_field.shape
    slabs = columns // LANES
    depths = slice_owner.shape[0]
    halos = [SWEEPS * (depths - d) for d in range(depths)]
    starts = [sum(halos[:d]) for d in range(depths)]
    halo = halos[0]
    own_columns = region_map.shape[1]
    swap_a = functools.partial(lax.ppermute, axis_name=("freq", "tile"), perm=swaps(freqs, tiles, 0))
    swap_b = functools.partial(lax.ppermute, axis_name=("freq", "tile"), perm=swaps(freqs, tiles, 1))

    labels = region_map.reshape(-1, LANES)
    vel_rows = rows * slabs
    row = (slabs, LANES)
    own, send_a, send_b, gather, wanted = call(
        functools.partial(prepare_kernel, halo),
        [(4, rows) + row, (4, halo) + row, (4, halo) + row, (vel_rows + labels.shape[0], LANES), (depths, SUB, LANES)],
        smem=1,
        operands=5,
        name="prepare",
    )(
        slice_owner,
        tiled_rows(source_field[:, 0]),
        tiled_rows(receiver_field[:, 0]),
        tiled_rows(velocity_store[0]),
        labels,
    )
    field_a, field_b = swap_a(send_a), swap_b(send_b)
    gathered = from_all_freqs(gather, freqs)
    speeds, send_a, send_b = call(
        functools.partial(select_kernel, halos, starts),
        [(depths, rows) + row, (sum(halos),) + row, (sum(halos),) + row],
        operands=1 + len(gathered),
        name="select",
    )(on_chip(wanted), *map(on_chip, gathered))
    speed_a = swap_a(send_a)
    speed_b = swap_b(send_b)
    me = lax.axis_index("freq")
    labels = jnp.stack([x[vel_rows:, :] for x in gathered[:freqs]])
    labels = labels[jnp.arange(freqs, dtype=jnp.int32) ^ me].reshape(freqs, rows, own_columns)
    labels = jnp.swapaxes(labels, 0, 1).reshape((rows,) + row)
    table = (depths, rows) + row
    sines, cosines, ratios, keep_next, keep_prev = call(
        functools.partial(angles_kernel, freqs),
        [table, table, table, (rows,) + row, (rows,) + row],
        scratch=[(rows, slabs + 2 * SUB, LANES)],
        operands=2,
        name="angles",
    )(on_chip(speeds), on_chip(labels))
    extent = rows + 2 * halo
    padded = (4, extent, slabs + 2 * SUB, LANES)
    x, y, z, early = call(
        functools.partial(begin_kernel, freqs, tiles, halos),
        [padded] * 3 + [table],
        operands=6,
        name="begin",
    )(*map(on_chip, (own, field_a, field_b, sines, cosines, ratios)))
    _, _, _, waves, image = call(
        functools.partial(march_kernel, freqs, tiles, halos, starts),
        [padded] * 3 + [(4, rows * slabs, LANES), (slabs * depths * rows, LANES)],
        scratch=[(extent,) + row, (rows, slabs + 2 * SUB, LANES)],
        operands=11,
        aliases={0: 0, 1: 1, 2: 2},
        name="march",
    )(
        *map(
            on_chip,
            (x, y, z, early, speed_a, speed_b, sines, cosines, ratios, keep_next, keep_prev),
        )
    )

    if own_columns == LANES:
        blocks = image.reshape(freqs, depths * rows, LANES)
    else:
        blocks = jnp.swapaxes(image.reshape(slabs, depths * rows, LANES), 0, 1)
        blocks = blocks.reshape(depths * rows, freqs, own_columns)
        blocks = jnp.swapaxes(blocks, 0, 1)
    smoothed = sum_over_freqs(blocks, freqs).reshape(depths, rows, own_columns)
    waves = untiled_rows(waves, rows, columns).reshape(2, 2, 1, rows, columns)
    return waves, smoothed


def solution(mesh):
    in_specs = (
        P(None, "freq", "tile", None),
        P(None, "freq", "tile", None),
        P("freq", "tile", None),
        P(),
        P("tile", "freq"),
    )
    out_specs = (P(None, None, "freq", "tile", None), P(None, "tile", "freq"))

    return jax.shard_map(on_device, mesh=mesh, in_specs=in_specs, out_specs=out_specs, check_vma=False)
```

```python
import functools
import math

import jax
import jax.numpy as jnp
from jax import lax
from jax.experimental import pallas as pl
from jax.experimental.pallas import tpu as pltpu
from jax.sharding import PartitionSpec as P


SWEEPS = 3
STEP_DEPTH = 4.0
SMOOTHING = 0.25
LANES = 128
SUB = 8
GAIN = 8.0
VMEM_LIMIT = 24 * 2**20


def tiled_rows(x):
    rows, columns = x.shape[-2:]
    lead = x.shape[:-2]
    x = x.reshape(lead + (rows // SUB, SUB, columns // LANES, LANES))
    return jnp.swapaxes(x, -3, -2).reshape(lead + (-1, LANES))


def untiled_rows(x, rows, columns):
    lead = x.shape[:-2]
    x = x.reshape(lead + (rows // SUB, columns // LANES, SUB, LANES))
    return jnp.swapaxes(x, -3, -2).reshape(lead + (rows, columns))


def tiled_row(r, slabs):
    return pl.ds((r // SUB) * SUB * slabs + r % SUB, slabs, stride=SUB)


def prepare_kernel(halo, owner, src, rcv, vel, lab, own, send_a, send_b, gather, wanted):
    _, rows, slabs, _ = own.shape
    me = lax.axis_index("freq")
    for d in range(wanted.shape[0]):
        wanted[d] = jnp.full(wanted.shape[1:], (owner[d] ^ me).astype(jnp.float32))
    for c in range(4):
        field = (src, rcv)[c // 2]
        for r in range(rows):
            own[c, r] = field[c % 2, tiled_row(r, slabs), :]
    even = lax.rem(lax.axis_index("tile"), 2) == 0
    a0 = jnp.where(even, rows - halo, 0)
    b0 = jnp.where(even, 0, rows - halo)
    for c in range(4):
        send_a[c] = own[c, pl.ds(a0, halo)]
        send_b[c] = own[c, pl.ds(b0, halo)]
    gather[: rows * slabs, :] = vel[...]
    gather[rows * slabs :, :] = lab[...].astype(jnp.float32)


def select_kernel(halos, starts, wanted, *refs):
    slices, (speeds, send_a, send_b) = refs[:-3], refs[-3:]
    _, rows, slabs, _ = speeds.shape
    even = lax.rem(lax.axis_index("tile"), 2) == 0
    for d, h in enumerate(halos):
        want = wanted[d, :slabs, :]
        values = [slices[0][tiled_row(r, slabs), :] for r in range(rows)]
        for k in range(1, len(slices)):
            hit = want == float(k)
            values = [
                jnp.where(hit, slices[k][tiled_row(r, slabs), :], v) for r, v in enumerate(values)
            ]
        for r, value in enumerate(values):
            speeds[d, r] = value
        a0 = jnp.where(even, rows - h, 0)
        b0 = jnp.where(even, 0, rows - h)
        send_a[starts[d] : starts[d] + h] = speeds[d, pl.ds(a0, h)]
        send_b[starts[d] : starts[d] + h] = speeds[d, pl.ds(b0, h)]


def omega_here(freqs):
    return 1.0 + lax.axis_index("freq").astype(jnp.float32) * (1.0 / freqs)


def sin_cos(x, scale):
    quarter = jnp.floor(x * (2.0 / math.pi) + 0.5)
    r = x - quarter * 1.5703125
    r = r - quarter * 4.838267948966192e-4
    z = r * r
    s = r + r * z * (-1.6666654611e-1 + z * (8.3321608736e-3 - z * 1.9515295891e-4))
    c = 1.0 - z * (
        0.5
        - z * (4.166664568298827e-2 - z * (1.388731625493765e-3 - z * 2.443315711809948e-5))
    )
    q = quarter.astype(jnp.int32)
    odd = (q & 1) == 1
    sine = jnp.where(odd, c, s) * jnp.where((q & 2) == 2, -scale, scale)
    cosine = jnp.where(odd, s, c) * jnp.where(((q + 1) & 2) == 2, -scale, scale)
    return sine, cosine


def depth_scale(d):
    return 1.0 if d == 0 else GAIN**-SWEEPS


def angles_kernel(freqs, speeds, labels, sines, cosines, ratios, keep_next, keep_prev, pad):
    depths, rows, slabs, _ = speeds.shape
    omega = omega_here(freqs)
    for d in range(depths):

        def row(i, carry, d=d):
            v = speeds[d, pl.ds(i * 4, 4)]
            s, c = sin_cos(omega * STEP_DEPTH / v, depth_scale(d))
            sines[d, pl.ds(i * 4, 4)] = s
            cosines[d, pl.ds(i * 4, 4)] = c
            ratios[d, pl.ds(i * 4, 4)] = v / omega
            return carry

        lax.fori_loop(0, rows // 4, row, 0, unroll=2)
    pad[...] = jnp.zeros_like(pad)
    mid = labels[...] + 1.0
    pad[:, SUB : SUB + slabs, :] = mid
    after, before = shifted(pad, slice(None))
    keep_next[...] = jnp.where(after == mid, SMOOTHING, 0.0)
    keep_prev[...] = jnp.where(before == mid, SMOOTHING, 0.0)


def shifted(pad, rows):
    slabs = pad.shape[-2] - 2 * SUB
    here = pad[rows, SUB : SUB + slabs, :]
    lane = lax.broadcasted_iota(jnp.int32, here.shape, 2)
    after = jnp.where(lane == 0, pad[rows, SUB + 1 : SUB + 1 + slabs, :], here)
    before = jnp.where(lane == LANES - 1, pad[rows, SUB - 1 : SUB - 1 + slabs, :], here)
    return pltpu.roll(after, LANES - 1, 2), pltpu.roll(before, 1, 2)


def rotate(src, dst, e, n, s, c):
    slabs = src.shape[-2] - 2 * SUB
    mid = slice(SUB, SUB + slabs)
    s0, s1, r0, r1 = (src[k, pl.ds(e, n), mid, :] for k in range(4))
    dst[0, pl.ds(e, n), mid, :] = s0 * c - s1 * s
    dst[1, pl.ds(e, n), mid, :] = s0 * s + s1 * c
    dst[2, pl.ds(e, n), mid, :] = r0 * c + r1 * s
    dst[3, pl.ds(e, n), mid, :] = r1 * c - r0 * s


def sweep_rows(src, dst, ratio_of, lo, hi):
    n = 2
    slabs = src.shape[-2] - 2 * SUB
    mid = slice(SUB, SUB + slabs)

    def chunk(e):
        ratio = ratio_of(e, n)
        for pair, sign in ((0, 1.0), (2, -1.0)):
            spread, total = [], []
            for c in (pair, pair + 1):
                here = src.at[c]
                q = here[pl.ds(e, n), mid, :] * 4.0
                after, before = shifted(here, pl.ds(e, n))
                around = (here[pl.ds(e + 1, n), mid, :] + here[pl.ds(e - 1, n), mid, :]) + (
                    after + before
                )
                spread.append(around - q)
                total.append(around + q)
            if sign > 0:
                first = total[0] - ratio * spread[1]
                second = total[1] + ratio * spread[0]
            else:
                first = total[0] + ratio * spread[1]
                second = total[1] - ratio * spread[0]
            dst[pair, pl.ds(e, n), mid, :] = first
            dst[pair + 1, pl.ds(e, n), mid, :] = second

    for e in range(lo, hi, n):
        chunk(min(e, hi - n))


def image_term(y, lo, hi, freqs):
    slabs = y.shape[-2] - 2 * SUB
    norm = GAIN ** (-2 * SWEEPS) / math.sqrt(freqs)
    s0, s1, r0, r1 = (y[c, lo:hi, SUB : SUB + slabs, :] for c in range(4))
    return (s0 * r0 + s1 * r1) * norm


def begin_kernel(
    freqs, tiles, halos, own, field_a, field_b, sines, cosines, ratios, x, y, z, early
):
    _, rows, slabs, _ = own.shape
    halo = halos[0]
    high0 = halo + rows
    extent = high0 + halo
    mid = slice(SUB, SUB + slabs)
    tile = lax.axis_index("tile")
    even = lax.rem(tile, 2) == 0
    low_in = jnp.where(tile == 0, 0.0, 1.0)
    high_in = jnp.where(tile == tiles - 1, 0.0, 1.0)

    for buf in (x, y, z):
        for c in range(4):
            buf[c, :, :SUB, :] = jnp.zeros((extent, SUB, LANES), jnp.float32)
            buf[c, :, SUB + slabs :, :] = jnp.zeros((extent, SUB, LANES), jnp.float32)

    def unpack(low, high):
        for c in range(4):
            y[c, 0:halo, mid, :] = low[c] * low_in
            y[c, high0:extent, mid, :] = high[c] * high_in

    @pl.when(even)
    def _():
        unpack(field_b, field_a)

    @pl.when(jnp.logical_not(even))
    def _():
        unpack(field_a, field_b)

    for c in range(4):
        y[c, halo:high0, mid, :] = own[c]

    for d in range(len(halos)):
        k = d * SWEEPS
        turned = (x, z)[d % 2]
        if 2 * k >= rows:
            break
        for r in range(k, rows - k, 2):
            at = slice(r, r + 2)
            rotate(y, turned, halo + r, 2, sines[d, at], cosines[d, at])
        for src, dst in ((turned, y), (y, turned), (turned, y)):
            k += 1
            if 2 * k < rows:
                ratio_of = lambda e, n, d=d: ratios[d, pl.ds(e - halo, n)]
                sweep_rows(src, dst, ratio_of, halo + k, high0 - k)
        if 2 * k < rows:
            early[d, k : rows - k] = image_term(y, halo + k, high0 - k, freqs)


def march_kernel(
    freqs, tiles, halos, starts,
    x_in, y_in, z_in, early, speed_a, speed_b, sines, cosines, ratios, keep_next, keep_prev,
    x, y, z, waves, image,
    coef, term,
):
    _, rows, slabs, _ = sines.shape
    depths = len(halos)
    halo = halos[0]
    high0 = halo + rows
    extent = high0 + halo
    mid = slice(SUB, SUB + slabs)
    tile = lax.axis_index("tile")
    even = lax.rem(tile, 2) == 0
    at_low = tile == 0
    at_high = tile == tiles - 1
    omega = omega_here(freqs)
    low_in = jnp.where(at_low, 0.0, 1.0)
    high_in = jnp.where(at_high, 0.0, 1.0)
    term[...] = jnp.zeros_like(term)

    def sweep(src, dst, k):
        ratio_of = lambda e, n: coef[pl.ds(e, n)]
        if 2 * k < rows:
            sweep_rows(src, dst, ratio_of, k, halo + k)
            sweep_rows(src, dst, ratio_of, high0 - k, extent - k)
        else:
            sweep_rows(src, dst, ratio_of, k, extent - k)
        for c in range(4):
            dst[c, halo - 1, mid, :] = dst[c, halo - 1, mid, :] * low_in
            dst[c, high0, mid, :] = dst[c, high0, mid, :] * high_in

    for d, h in enumerate(halos):
        scale = depth_scale(d)
        turned = (x, z)[d % 2]

        def halo_rows(i, carry, d=d, h=h, scale=scale, turned=turned):
            a = speed_a[starts[d] + i]
            b = speed_b[starts[d] + i]
            for low in (True, False):
                v = jnp.where(even, b, a) if low else jnp.where(even, a, b)
                v = jnp.where(at_low if low else at_high, 1.0, v)
                e = halo - h + i if low else high0 + i
                s, c = sin_cos(omega * STEP_DEPTH / v, scale)
                coef[e] = v / omega
                rotate(y, turned, e, 1, s[None], c[None])
            return carry

        lax.fori_loop(0, h, halo_rows, 0, unroll=True)
        coef[halo:high0] = ratios[d]
        k = d * SWEEPS
        for r in range(rows):
            if r < k or r >= rows - k:
                rotate(y, turned, halo + r, 1, sines[d, r : r + 1], cosines[d, r : r + 1])

        sweep(turned, y, k + 1)
        sweep(y, turned, k + 2)
        sweep(turned, y, k + 3)

        k += SWEEPS
        if 2 * k < rows:
            term[:k, mid, :] = image_term(y, halo, halo + k, freqs)
            term[k : rows - k, mid, :] = early[d, k : rows - k]
            term[rows - k :, mid, :] = image_term(y, high0 - k, high0, freqs)
        else:
            term[:, mid, :] = image_term(y, halo, high0, freqs)
        here = term[:, mid, :]
        after, before = shifted(term, slice(None))
        smooth = here + (keep_next[...] * (after - here) + keep_prev[...] * (before - here))
        for r in range(rows):
            image[pl.ds(d * rows + r, slabs, stride=depths * rows), :] = smooth[r]

    for c in range(4):
        for r in range(rows):
            waves[c, tiled_row(r, slabs), :] = y[c, halo + r, mid, :] * GAIN**-SWEEPS


def swaps(freqs, tiles, first):
    pairs = []
    for t in range(tiles):
        u = t + 1 if (t - first) % 2 == 0 else t - 1
        for f in range(freqs):
            g = f
            if not 0 <= u < tiles:
                g = min(f ^ 1, freqs - 1)
            pairs.append((f * tiles + t, g * tiles + (u if 0 <= u < tiles else t)))
    return pairs


def from_all_freqs(x, freqs):
    if freqs & (freqs - 1):
        whole = lax.all_gather(x, "freq")
        me = lax.axis_index("freq")
        return [jnp.take(whole, jnp.minimum(me ^ k, freqs - 1), axis=0) for k in range(2 * freqs)]

    def swap(value, bits):
        return lax.ppermute(value, "freq", [(i, i ^ bits) for i in range(freqs)])

    near = [x]
    for k in range(2, freqs, 2):
        near.append(swap(x, k))
    return [v for x in near for v in (x, swap(x, 1))]


def sum_over_freqs(blocks, freqs):
    if freqs % 2 or freqs & (freqs - 1):
        return lax.psum_scatter(blocks, "freq", scatter_dimension=0, tiled=False)
    me = lax.axis_index("freq")
    core, chip = lax.rem(me, 2), me // 2

    def swap(value, bits):
        return lax.ppermute(value, "freq", [(i, i ^ bits) for i in range(freqs)])

    blocks = blocks.reshape((freqs // 2, 2) + blocks.shape[1:])
    kept = lax.dynamic_index_in_dim(blocks, core, 1, keepdims=False)
    sent = lax.dynamic_index_in_dim(blocks, 1 - core, 1, keepdims=False)
    kept = kept + swap(sent, 1)
    total = lax.dynamic_index_in_dim(kept, chip, 0, keepdims=False)
    others = []
    for m in range(1, freqs // 2):
        others.append(swap(lax.dynamic_index_in_dim(kept, chip ^ m, 0, keepdims=False), 2 * m))
    for other in others:
        total = total + other
    return total


def on_chip(x):
    return pltpu.with_memory_space_constraint(x, pltpu.VMEM)


def call(kernel, out, scratch=(), name=None, smem=0, operands=0, aliases=None):
    specs = [pl.BlockSpec(memory_space=pltpu.SMEM)] * smem
    specs += [pl.BlockSpec(memory_space=pltpu.VMEM)] * (operands - smem)
    return pl.pallas_call(
        kernel,
        out_shape=[pltpu.VMEM(s, jnp.float32) for s in out],
        in_specs=specs,
        out_specs=[pl.BlockSpec(memory_space=pltpu.VMEM)] * len(out),
        scratch_shapes=[pltpu.VMEM(s, jnp.float32) for s in scratch],
        input_output_aliases=aliases or {},
        compiler_params=None if name == 'prepare' else pltpu.CompilerParams(vmem_limit_bytes=VMEM_LIMIT),
    )


def on_device(source_field, receiver_field, velocity_store, slice_owner, region_map):
    freqs, tiles = lax.axis_size("freq"), lax.axis_size("tile")
    _, _, rows, columns = source_field.shape
    slabs = columns // LANES
    depths = slice_owner.shape[0]
    halos = [SWEEPS * (depths - d) for d in range(depths)]
    starts = [sum(halos[:d]) for d in range(depths)]
    halo = halos[0]
    own_columns = region_map.shape[1]
    swap_a = functools.partial(lax.ppermute, axis_name=("freq", "tile"), perm=swaps(freqs, tiles, 0))
    swap_b = functools.partial(lax.ppermute, axis_name=("freq", "tile"), perm=swaps(freqs, tiles, 1))

    labels = region_map.reshape(-1, LANES)
    vel_rows = rows * slabs
    row = (slabs, LANES)
    own, send_a, send_b, gather, wanted = call(
        functools.partial(prepare_kernel, halo),
        [(4, rows) + row, (4, halo) + row, (4, halo) + row, (vel_rows + labels.shape[0], LANES), (depths, SUB, LANES)],
        smem=1,
        operands=5,
        name="prepare",
    )(
        slice_owner,
        tiled_rows(source_field[:, 0]),
        tiled_rows(receiver_field[:, 0]),
        tiled_rows(velocity_store[0]),
        labels,
    )
    field_a, field_b = swap_a(send_a), swap_b(send_b)
    gathered = from_all_freqs(gather, freqs)
    speeds, send_a, send_b = call(
        functools.partial(select_kernel, halos, starts),
        [(depths, rows) + row, (sum(halos),) + row, (sum(halos),) + row],
        operands=1 + len(gathered),
        name="select",
    )(on_chip(wanted), *map(on_chip, gathered))
    speed_a = swap_a(send_a)
    speed_b = swap_b(send_b)
    me = lax.axis_index("freq")
    labels = jnp.stack([x[vel_rows:, :] for x in gathered[:freqs]])
    labels = labels[jnp.arange(freqs, dtype=jnp.int32) ^ me].reshape(freqs, rows, own_columns)
    labels = jnp.swapaxes(labels, 0, 1).reshape((rows,) + row)
    table = (depths, rows) + row
    sines, cosines, ratios, keep_next, keep_prev = call(
        functools.partial(angles_kernel, freqs),
        [table, table, table, (rows,) + row, (rows,) + row],
        scratch=[(rows, slabs + 2 * SUB, LANES)],
        operands=2,
        name="angles",
    )(on_chip(speeds), on_chip(labels))
    extent = rows + 2 * halo
    padded = (4, extent, slabs + 2 * SUB, LANES)
    x, y, z, early = call(
        functools.partial(begin_kernel, freqs, tiles, halos),
        [padded] * 3 + [table],
        operands=6,
        name="begin",
    )(*map(on_chip, (own, field_a, field_b, sines, cosines, ratios)))
    _, _, _, waves, image = call(
        functools.partial(march_kernel, freqs, tiles, halos, starts),
        [padded] * 3 + [(4, rows * slabs, LANES), (slabs * depths * rows, LANES)],
        scratch=[(extent,) + row, (rows, slabs + 2 * SUB, LANES)],
        operands=11,
        aliases={0: 0, 1: 1, 2: 2},
        name="march",
    )(
        *map(
            on_chip,
            (x, y, z, early, speed_a, speed_b, sines, cosines, ratios, keep_next, keep_prev),
        )
    )

    if own_columns == LANES:
        blocks = image.reshape(freqs, depths * rows, LANES)
    else:
        blocks = jnp.swapaxes(image.reshape(slabs, depths * rows, LANES), 0, 1)
        blocks = blocks.reshape(depths * rows, freqs, own_columns)
        blocks = jnp.swapaxes(blocks, 0, 1)
    smoothed = sum_over_freqs(blocks, freqs).reshape(depths, rows, own_columns)
    waves = untiled_rows(waves, rows, columns).reshape(2, 2, 1, rows, columns)
    return waves, smoothed


def solution(mesh):
    in_specs = (
        P(None, "freq", "tile", None),
        P(None, "freq", "tile", None),
        P("freq", "tile", None),
        P(),
        P("tile", "freq"),
    )
    out_specs = (P(None, None, "freq", "tile", None), P(None, "tile", "freq"))

    return jax.shard_map(on_device, mesh=mesh, in_specs=in_specs, out_specs=out_specs, check_vma=False)
```

```python
import functools
import math

import jax
import jax.numpy as jnp
from jax import lax
from jax.experimental import pallas as pl
from jax.experimental.pallas import tpu as pltpu
from jax.sharding import PartitionSpec as P


SWEEPS = 3
STEP_DEPTH = 4.0
SMOOTHING = 0.25
LANES = 128
SUB = 8
GAIN = 8.0
VMEM_LIMIT = 24 * 2**20


def tiled_rows(x):
    rows, columns = x.shape[-2:]
    lead = x.shape[:-2]
    x = x.reshape(lead + (rows // SUB, SUB, columns // LANES, LANES))
    return jnp.swapaxes(x, -3, -2).reshape(lead + (-1, LANES))


def untiled_rows(x, rows, columns):
    lead = x.shape[:-2]
    x = x.reshape(lead + (rows // SUB, columns // LANES, SUB, LANES))
    return jnp.swapaxes(x, -3, -2).reshape(lead + (rows, columns))


def tiled_row(r, slabs):
    return pl.ds((r // SUB) * SUB * slabs + r % SUB, slabs, stride=SUB)


def prepare_kernel(halo, owner, src, rcv, vel, lab, own, send_a, send_b, gather, wanted):
    _, rows, slabs, _ = own.shape
    me = lax.axis_index("freq")
    for d in range(wanted.shape[0]):
        wanted[d] = jnp.full(wanted.shape[1:], (owner[d] ^ me).astype(jnp.float32))
    for c in range(4):
        field = (src, rcv)[c // 2]
        for r in range(rows):
            own[c, r] = field[c % 2, tiled_row(r, slabs), :]
    even = lax.rem(lax.axis_index("tile"), 2) == 0
    a0 = jnp.where(even, rows - halo, 0)
    b0 = jnp.where(even, 0, rows - halo)
    for c in range(4):
        send_a[c] = own[c, pl.ds(a0, halo)]
        send_b[c] = own[c, pl.ds(b0, halo)]
    gather[: rows * slabs, :] = vel[...]
    gather[rows * slabs :, :] = lab[...].astype(jnp.float32)


def select_kernel(halos, starts, wanted, *refs):
    slices, (speeds, send_a, send_b) = refs[:-3], refs[-3:]
    _, rows, slabs, _ = speeds.shape
    even = lax.rem(lax.axis_index("tile"), 2) == 0
    for d, h in enumerate(halos):
        want = wanted[d, :slabs, :]
        values = [slices[0][tiled_row(r, slabs), :] for r in range(rows)]
        for k in range(1, len(slices)):
            hit = want == float(k)
            values = [
                jnp.where(hit, slices[k][tiled_row(r, slabs), :], v) for r, v in enumerate(values)
            ]
        for r, value in enumerate(values):
            speeds[d, r] = value
        a0 = jnp.where(even, rows - h, 0)
        b0 = jnp.where(even, 0, rows - h)
        send_a[starts[d] : starts[d] + h] = speeds[d, pl.ds(a0, h)]
        send_b[starts[d] : starts[d] + h] = speeds[d, pl.ds(b0, h)]


def omega_here(freqs):
    return 1.0 + lax.axis_index("freq").astype(jnp.float32) * (1.0 / freqs)


def sin_cos(x, scale):
    quarter = jnp.floor(x * (2.0 / math.pi) + 0.5)
    r = x - quarter * 1.5703125
    r = r - quarter * 4.838267948966192e-4
    z = r * r
    s = r + r * z * (-1.6666654611e-1 + z * (8.3321608736e-3 - z * 1.9515295891e-4))
    c = 1.0 - z * (
        0.5
        - z * (4.166664568298827e-2 - z * (1.388731625493765e-3 - z * 2.443315711809948e-5))
    )
    q = quarter.astype(jnp.int32)
    odd = (q & 1) == 1
    sine = jnp.where(odd, c, s) * jnp.where((q & 2) == 2, -scale, scale)
    cosine = jnp.where(odd, s, c) * jnp.where(((q + 1) & 2) == 2, -scale, scale)
    return sine, cosine


def depth_scale(d):
    return 1.0 if d == 0 else GAIN**-SWEEPS


def angles_kernel(freqs, offset, speeds, *refs):
    labels, (sines, cosines, ratios, keep_next, keep_prev, pad) = refs[:-6], refs[-6:]
    depths, rows, slabs, _ = speeds.shape
    omega = omega_here(freqs)
    for d in range(depths):

        def row(i, carry, d=d):
            v = speeds[d, pl.ds(i * 4, 4)]
            s, c = sin_cos(omega * STEP_DEPTH / v, depth_scale(d))
            sines[d, pl.ds(i * 4, 4)] = s
            cosines[d, pl.ds(i * 4, 4)] = c
            ratios[d, pl.ds(i * 4, 4)] = v / omega
            return carry

        lax.fori_loop(0, rows // 4, row, 0, unroll=2)
    pad[...] = jnp.zeros_like(pad)
    if offset:
        me = lax.axis_index("freq")
        blocks = [x[offset:, :] for x in labels]
        bit = 1
        while bit < slabs:
            flip = (me & bit) != 0
            blocks = [jnp.where(flip, blocks[k ^ bit], blocks[k]) for k in range(slabs)]
            bit *= 2
        for k, block in enumerate(blocks):
            pad[:, SUB + k, :] = block + 1.0
    else:
        pad[:, SUB : SUB + slabs, :] = labels[0][...] + 1.0
    mid = pad[:, SUB : SUB + slabs, :]
    after, before = shifted(pad, slice(None))
    keep_next[...] = jnp.where(after == mid, SMOOTHING, 0.0)
    keep_prev[...] = jnp.where(before == mid, SMOOTHING, 0.0)


def shifted(pad, rows):
    slabs = pad.shape[-2] - 2 * SUB
    here = pad[rows, SUB : SUB + slabs, :]
    lane = lax.broadcasted_iota(jnp.int32, here.shape, 2)
    after = jnp.where(lane == 0, pad[rows, SUB + 1 : SUB + 1 + slabs, :], here)
    before = jnp.where(lane == LANES - 1, pad[rows, SUB - 1 : SUB - 1 + slabs, :], here)
    return pltpu.roll(after, LANES - 1, 2), pltpu.roll(before, 1, 2)


def rotate(src, dst, e, n, s, c):
    slabs = src.shape[-2] - 2 * SUB
    mid = slice(SUB, SUB + slabs)
    s0, s1, r0, r1 = (src[k, pl.ds(e, n), mid, :] for k in range(4))
    dst[0, pl.ds(e, n), mid, :] = s0 * c - s1 * s
    dst[1, pl.ds(e, n), mid, :] = s0 * s + s1 * c
    dst[2, pl.ds(e, n), mid, :] = r0 * c + r1 * s
    dst[3, pl.ds(e, n), mid, :] = r1 * c - r0 * s


def sweep_rows(src, dst, ratio_of, lo, hi):
    n = 1
    slabs = src.shape[-2] - 2 * SUB
    mid = slice(SUB, SUB + slabs)

    def chunk(e):
        ratio = ratio_of(e, n)
        for pair, sign in ((0, 1.0), (2, -1.0)):
            spread, total = [], []
            for c in (pair, pair + 1):
                here = src.at[c]
                q = here[pl.ds(e, n), mid, :] * 4.0
                after, before = shifted(here, pl.ds(e, n))
                around = (here[pl.ds(e + 1, n), mid, :] + here[pl.ds(e - 1, n), mid, :]) + (
                    after + before
                )
                spread.append(around - q)
                total.append(around + q)
            if sign > 0:
                first = total[0] - ratio * spread[1]
                second = total[1] + ratio * spread[0]
            else:
                first = total[0] + ratio * spread[1]
                second = total[1] - ratio * spread[0]
            dst[pair, pl.ds(e, n), mid, :] = first
            dst[pair + 1, pl.ds(e, n), mid, :] = second

    for e in range(lo, hi, n):
        chunk(min(e, hi - n))


def image_term(y, lo, hi, freqs):
    slabs = y.shape[-2] - 2 * SUB
    norm = GAIN ** (-2 * SWEEPS) / math.sqrt(freqs)
    s0, s1, r0, r1 = (y[c, lo:hi, SUB : SUB + slabs, :] for c in range(4))
    return (s0 * r0 + s1 * r1) * norm


def begin_kernel(
    freqs, tiles, halos, own, field_a, field_b, sines, cosines, ratios, x, y, z, early
):
    _, rows, slabs, _ = own.shape
    halo = halos[0]
    high0 = halo + rows
    extent = high0 + halo
    mid = slice(SUB, SUB + slabs)
    tile = lax.axis_index("tile")
    even = lax.rem(tile, 2) == 0
    low_in = jnp.where(tile == 0, 0.0, 1.0)
    high_in = jnp.where(tile == tiles - 1, 0.0, 1.0)

    for buf in (x, y, z):
        for c in range(4):
            buf[c, :, :SUB, :] = jnp.zeros((extent, SUB, LANES), jnp.float32)
            buf[c, :, SUB + slabs :, :] = jnp.zeros((extent, SUB, LANES), jnp.float32)

    def unpack(low, high):
        for c in range(4):
            y[c, 0:halo, mid, :] = low[c] * low_in
            y[c, high0:extent, mid, :] = high[c] * high_in

    @pl.when(even)
    def _():
        unpack(field_b, field_a)

    @pl.when(jnp.logical_not(even))
    def _():
        unpack(field_a, field_b)

    for c in range(4):
        y[c, halo:high0, mid, :] = own[c]

    for d in range(len(halos)):
        k = d * SWEEPS
        turned = (x, z)[d % 2]
        if 2 * k >= rows:
            break
        for r in range(k, rows - k, 2):
            at = slice(r, r + 2)
            rotate(y, turned, halo + r, 2, sines[d, at], cosines[d, at])
        for src, dst in ((turned, y), (y, turned), (turned, y)):
            k += 1
            if 2 * k < rows:
                ratio_of = lambda e, n, d=d: ratios[d, pl.ds(e - halo, n)]
                sweep_rows(src, dst, ratio_of, halo + k, high0 - k)
        if 2 * k < rows:
            early[d, k : rows - k] = image_term(y, halo + k, high0 - k, freqs)


def march_kernel(
    freqs, tiles, halos, starts,
    x_in, y_in, z_in, early, speed_a, speed_b, sines, cosines, ratios, keep_next, keep_prev,
    x, y, z, waves, image,
    coef, term,
):
    _, rows, slabs, _ = sines.shape
    depths = len(halos)
    halo = halos[0]
    high0 = halo + rows
    extent = high0 + halo
    mid = slice(SUB, SUB + slabs)
    tile = lax.axis_index("tile")
    even = lax.rem(tile, 2) == 0
    at_low = tile == 0
    at_high = tile == tiles - 1
    omega = omega_here(freqs)
    low_in = jnp.where(at_low, 0.0, 1.0)
    high_in = jnp.where(at_high, 0.0, 1.0)
    term[...] = jnp.zeros_like(term)

    def sweep(src, dst, k):
        ratio_of = lambda e, n: coef[pl.ds(e, n)]
        if 2 * k < rows:
            sweep_rows(src, dst, ratio_of, k, halo + k)
            sweep_rows(src, dst, ratio_of, high0 - k, extent - k)
        else:
            sweep_rows(src, dst, ratio_of, k, extent - k)
        for c in range(4):
            dst[c, halo - 1, mid, :] = dst[c, halo - 1, mid, :] * low_in
            dst[c, high0, mid, :] = dst[c, high0, mid, :] * high_in

    for d, h in enumerate(halos):
        scale = depth_scale(d)
        turned = (x, z)[d % 2]

        def halo_rows(i, carry, d=d, h=h, scale=scale, turned=turned):
            a = speed_a[starts[d] + i]
            b = speed_b[starts[d] + i]
            for low in (True, False):
                v = jnp.where(even, b, a) if low else jnp.where(even, a, b)
                v = jnp.where(at_low if low else at_high, 1.0, v)
                e = halo - h + i if low else high0 + i
                s, c = sin_cos(omega * STEP_DEPTH / v, scale)
                coef[e] = v / omega
                rotate(y, turned, e, 1, s[None], c[None])
            return carry

        lax.fori_loop(0, h, halo_rows, 0, unroll=True)
        coef[halo:high0] = ratios[d]
        k = d * SWEEPS
        for r in range(rows):
            if r < k or r >= rows - k:
                rotate(y, turned, halo + r, 1, sines[d, r : r + 1], cosines[d, r : r + 1])

        sweep(turned, y, k + 1)
        sweep(y, turned, k + 2)
        sweep(turned, y, k + 3)

        k += SWEEPS
        if 2 * k < rows:
            term[:k, mid, :] = image_term(y, halo, halo + k, freqs)
            term[k : rows - k, mid, :] = early[d, k : rows - k]
            term[rows - k :, mid, :] = image_term(y, high0 - k, high0, freqs)
        else:
            term[:, mid, :] = image_term(y, halo, high0, freqs)
        here = term[:, mid, :]
        after, before = shifted(term, slice(None))
        smooth = here + (keep_next[...] * (after - here) + keep_prev[...] * (before - here))
        for r in range(rows):
            image[pl.ds(d * rows + r, slabs, stride=depths * rows), :] = smooth[r]

    for c in range(4):
        for r in range(rows):
            waves[c, tiled_row(r, slabs), :] = y[c, halo + r, mid, :] * GAIN**-SWEEPS


def swaps(freqs, tiles, first):
    pairs = []
    for t in range(tiles):
        u = t + 1 if (t - first) % 2 == 0 else t - 1
        for f in range(freqs):
            g = f
            if not 0 <= u < tiles:
                g = min(f ^ 1, freqs - 1)
            pairs.append((f * tiles + t, g * tiles + (u if 0 <= u < tiles else t)))
    return pairs


def from_all_freqs(x, freqs):
    if freqs & (freqs - 1):
        whole = lax.all_gather(x, "freq")
        me = lax.axis_index("freq")
        return [jnp.take(whole, jnp.minimum(me ^ k, freqs - 1), axis=0) for k in range(2 * freqs)]

    def swap(value, bits):
        return lax.ppermute(value, "freq", [(i, i ^ bits) for i in range(freqs)])

    near = [x]
    for k in range(2, freqs, 2):
        near.append(swap(x, k))
    return [v for x in near for v in (x, swap(x, 1))]


def sum_over_freqs(blocks, freqs):
    if freqs % 2 or freqs & (freqs - 1):
        return lax.psum_scatter(blocks, "freq", scatter_dimension=0, tiled=False)
    me = lax.axis_index("freq")
    core, chip = lax.rem(me, 2), me // 2

    def swap(value, bits):
        return lax.ppermute(value, "freq", [(i, i ^ bits) for i in range(freqs)])

    blocks = blocks.reshape((freqs // 2, 2) + blocks.shape[1:])
    kept = lax.dynamic_index_in_dim(blocks, core, 1, keepdims=False)
    sent = lax.dynamic_index_in_dim(blocks, 1 - core, 1, keepdims=False)
    kept = kept + swap(sent, 1)
    total = lax.dynamic_index_in_dim(kept, chip, 0, keepdims=False)
    others = []
    for m in range(1, freqs // 2):
        others.append(swap(lax.dynamic_index_in_dim(kept, chip ^ m, 0, keepdims=False), 2 * m))
    for other in others:
        total = total + other
    return total


def on_chip(x):
    return pltpu.with_memory_space_constraint(x, pltpu.VMEM)


def call(kernel, out, scratch=(), name=None, smem=0, operands=0, aliases=None):
    specs = [pl.BlockSpec(memory_space=pltpu.SMEM)] * smem
    specs += [pl.BlockSpec(memory_space=pltpu.VMEM)] * (operands - smem)
    return pl.pallas_call(
        kernel,
        out_shape=[pltpu.VMEM(s, jnp.float32) for s in out],
        in_specs=specs,
        out_specs=[pl.BlockSpec(memory_space=pltpu.VMEM)] * len(out),
        scratch_shapes=[pltpu.VMEM(s, jnp.float32) for s in scratch],
        input_output_aliases=aliases or {},
        compiler_params=None if name == 'prepare' else pltpu.CompilerParams(vmem_limit_bytes=VMEM_LIMIT),
    )


def on_device(source_field, receiver_field, velocity_store, slice_owner, region_map):
    freqs, tiles = lax.axis_size("freq"), lax.axis_size("tile")
    _, _, rows, columns = source_field.shape
    slabs = columns // LANES
    depths = slice_owner.shape[0]
    halos = [SWEEPS * (depths - d) for d in range(depths)]
    starts = [sum(halos[:d]) for d in range(depths)]
    halo = halos[0]
    own_columns = region_map.shape[1]
    swap_a = functools.partial(lax.ppermute, axis_name=("freq", "tile"), perm=swaps(freqs, tiles, 0))
    swap_b = functools.partial(lax.ppermute, axis_name=("freq", "tile"), perm=swaps(freqs, tiles, 1))

    labels = region_map.reshape(-1, LANES)
    vel_rows = rows * slabs
    row = (slabs, LANES)
    own, send_a, send_b, gather, wanted = call(
        functools.partial(prepare_kernel, halo),
        [(4, rows) + row, (4, halo) + row, (4, halo) + row, (vel_rows + labels.shape[0], LANES), (depths, SUB, LANES)],
        smem=1,
        operands=5,
        name="prepare",
    )(
        slice_owner,
        tiled_rows(source_field[:, 0]),
        tiled_rows(receiver_field[:, 0]),
        tiled_rows(velocity_store[0]),
        labels,
    )
    field_a, field_b = swap_a(send_a), swap_b(send_b)
    gathered = from_all_freqs(gather, freqs)
    speeds, send_a, send_b = call(
        functools.partial(select_kernel, halos, starts),
        [(depths, rows) + row, (sum(halos),) + row, (sum(halos),) + row],
        operands=1 + len(gathered),
        name="select",
    )(on_chip(wanted), *map(on_chip, gathered))
    speed_a = swap_a(send_a)
    speed_b = swap_b(send_b)
    if own_columns == LANES and freqs == slabs and freqs & (freqs - 1) == 0:
        offset, labels = vel_rows, gathered
    else:
        offset = 0
        me = lax.axis_index("freq")
        labels = jnp.stack([x[vel_rows:, :] for x in gathered[:freqs]])
        labels = labels[jnp.arange(freqs, dtype=jnp.int32) ^ me].reshape(freqs, rows, own_columns)
        labels = [jnp.swapaxes(labels, 0, 1).reshape((rows,) + row)]
    table = (depths, rows) + row
    sines, cosines, ratios, keep_next, keep_prev = call(
        functools.partial(angles_kernel, freqs, offset),
        [table, table, table, (rows,) + row, (rows,) + row],
        scratch=[(rows, slabs + 2 * SUB, LANES)],
        operands=1 + len(labels),
        name="angles",
    )(on_chip(speeds), *map(on_chip, labels))
    extent = rows + 2 * halo
    padded = (4, extent, slabs + 2 * SUB, LANES)
    x, y, z, early = call(
        functools.partial(begin_kernel, freqs, tiles, halos),
        [padded] * 3 + [table],
        operands=6,
        name="begin",
    )(*map(on_chip, (own, field_a, field_b, sines, cosines, ratios)))
    _, _, _, waves, image = call(
        functools.partial(march_kernel, freqs, tiles, halos, starts),
        [padded] * 3 + [(4, rows * slabs, LANES), (slabs * depths * rows, LANES)],
        scratch=[(extent,) + row, (rows, slabs + 2 * SUB, LANES)],
        operands=11,
        aliases={0: 0, 1: 1, 2: 2},
        name="march",
    )(
        *map(
            on_chip,
            (x, y, z, early, speed_a, speed_b, sines, cosines, ratios, keep_next, keep_prev),
        )
    )

    if own_columns == LANES:
        blocks = image.reshape(freqs, depths * rows, LANES)
    else:
        blocks = jnp.swapaxes(image.reshape(slabs, depths * rows, LANES), 0, 1)
        blocks = blocks.reshape(depths * rows, freqs, own_columns)
        blocks = jnp.swapaxes(blocks, 0, 1)
    smoothed = sum_over_freqs(blocks, freqs).reshape(depths, rows, own_columns)
    waves = untiled_rows(waves, rows, columns).reshape(2, 2, 1, rows, columns)
    return waves, smoothed


def solution(mesh):
    in_specs = (
        P(None, "freq", "tile", None),
        P(None, "freq", "tile", None),
        P("freq", "tile", None),
        P(),
        P("tile", "freq"),
    )
    out_specs = (P(None, None, "freq", "tile", None), P(None, "tile", "freq"))

    return jax.shard_map(on_device, mesh=mesh, in_specs=in_specs, out_specs=out_specs, check_vma=False)
```
